128 devices in a mesh: grid: 32 (over z, x, core), rep: 4 (over y).
Axes of the slice: x: 4, y: 4, z: 4, core: 2. Of those that a mesh axis runs over, the one named last changes fastest.
Arguments:
- functions: bfloat16 [8192, 32768], P(('grid', 'rep')), may hold values from -6 to 6
- filter_taps: bfloat16 [16], replicated, may hold values from -0.59765625 to 0.59765625
- potential: float32 [32768], replicated, may hold values from 0 to 1
- energies: float32 [8192], P(('grid', 'rep')), may hold values from -1.5 to -0.5
- region_start: int32 [8192], P(('grid', 'rep')), may hold values from 0 to 128
- region_length: int32 [8192], P(('grid', 'rep')), may hold values from 256 to 384
- partner_groups: int32 [128, 3], replicated, may hold values from 0 to 127, as said below
Outputs:
- corrected: bfloat16 [8192, 32768], P(('grid', 'rep'))
The draws below stay inside these ranges and needn't reach their ends.
Inputs may be any that keep to these rules, and one draw needn't show every extreme that they name: `partner_groups`: the 3 entries of a row are distinct and differ from the row's own group; each is the row's group plus an offset of magnitude 1 to 63, modulo 128.
All inputs are finite; a program needn't handle non-finite values.
Results may differ from the reference program's by a relative error of at most 0.005.
Values may be sent and summed in bfloat16 or wider, within the bound.
A program may use at most 128 MiB of HBM per device.

```python
import jax
import jax.numpy as jnp
from jax import lax

SIDE = 32
NC = 32768
BLOCK = 64
NB = 512
GROUP = 64
TAPS = 16
PARTNERS = 3
LMIN = 256
LMAX = 384
NF = 8192
NG = 128


def draw_partner_groups(key, part):
    half = (NG - 1) // 2
    upward = jnp.arange(1, half + 1, dtype=jnp.int32)
    offsets = jnp.concatenate([upward, -upward])
    subkeys = jax.random.split(key, NG)
    shuffled = jax.vmap(lambda subkey: jax.random.permutation(subkey, offsets))(subkeys)[:, :PARTNERS]
    without_minus = jnp.concatenate([upward, -upward[1:]])
    without_plus = jnp.concatenate([upward[1:], -upward])
    first_key = jax.random.fold_in(key, 7001)
    last_key = jax.random.fold_in(key, 7002)
    first_row = jnp.concatenate([jnp.array([-1], jnp.int32), jax.random.permutation(first_key, without_minus)[:PARTNERS - 1]])
    last_row = jnp.concatenate([jnp.array([1], jnp.int32), jax.random.permutation(last_key, without_plus)[:PARTNERS - 1]])
    shuffled = shuffled.at[0].set(first_row).at[NG - 1].set(last_row)
    return ((jnp.arange(NG, dtype=jnp.int32)[:, None] + shuffled) % NG).astype(jnp.int32)


def set_ends(entries, rng, low, high):
    longest = entries.shape.index(max(entries.shape))
    spots = []
    for shift in (0, 1):
        where = [jax.random.randint(jax.random.fold_in(rng, axis), (), 0, length) for axis, length in enumerate(entries.shape)]
        where[longest] = (where[longest] + shift) % entries.shape[longest]
        spots.append(tuple(where))
    return entries.at[spots[0]].set(low).at[spots[1]].set(high)


def steps_of(key, extent, cuts, least, high):
    def one(position, blocks):
        steps = jax.random.uniform(jax.random.fold_in(jax.random.fold_in(key, 6), position), (blocks,), jnp.float32, least / len(cuts), high / len(cuts))
        return jnp.repeat(jnp.exp(steps), extent[position] // blocks).reshape((-1,) + (1,) * (len(extent) - position - 1))

    loudness = one(*cuts[0])
    for cut in cuts[1:]:
        loudness = loudness * one(*cut)
    return loudness


def noise(rng, extent, deviation, reach, pieces=(), kind=jnp.bfloat16):
    entries = deviation * jax.random.normal(rng, extent, jnp.float32)
    if pieces:
        entries = entries * steps_of(rng, extent, pieces, -0.22, 0.18)
    return jnp.clip(entries, -reach, reach).astype(kind)


def setup_inputs(seed: int = 0) -> dict:
    key_list = jax.random.split(jax.random.key(seed), 8)
    functions = noise(key_list[0], (NF, NC), 1.0, 6.0, ((0, 128),))
    filter_taps = noise(key_list[1], (TAPS,), 0.1, 0.59765625)
    potential = jnp.clip(jax.random.uniform(key_list[2], (NC,), jnp.float32, 0.0, 1.0), 0.0, 1.0)
    energies = jnp.clip(-1.5 + 1.0 * jax.random.uniform(key_list[3], (NF,), jnp.float32) ** steps_of(key_list[3], (NF,), ((0, 128),), -0.2, 0.2), -1.5, -0.5)
    region_start = set_ends(jax.random.randint(key_list[4], (NF,), 0, NB - LMAX + 1), jax.random.fold_in(key_list[4], 1), 0, NB - LMAX).astype(jnp.int32)
    region_length = set_ends(jax.random.randint(key_list[5], (NF,), LMIN, LMAX + 1), jax.random.fold_in(key_list[5], 1), LMIN, LMAX).astype(jnp.int32)
    partner_groups = draw_partner_groups(jax.random.fold_in(key_list[7], 71), 0)
    return {"functions": functions, "filter_taps": filter_taps, "potential": potential, "energies": energies, "region_start": region_start, "region_length": region_length, "partner_groups": partner_groups}


def filter_along(values, taps, along_axis):
    centre = TAPS // 2
    widths = [(0, 0)] * values.ndim
    widths[along_axis] = (centre, TAPS - centre)
    padded = jnp.pad(values, widths)
    running = jnp.zeros(values.shape, jnp.float32)
    for offset in range(TAPS):
        running = running + taps[offset] * lax.slice_in_dim(padded, offset, offset + SIDE, axis=along_axis)
    return running


def reference(functions, filter_taps, potential, energies, region_start, region_length, partner_groups):
    taps = filter_taps.astype(jnp.float32)
    block_index = (jnp.arange(NC) // BLOCK).astype(jnp.int32)

    def refine(packed):
        rows, energy, first, count = packed
        values = rows.astype(jnp.float32)
        cube = values.reshape(GROUP, SIDE, SIDE, SIDE)
        kinetic = filter_along(cube, taps, 1) + filter_along(cube, taps, 2) + filter_along(cube, taps, 3)
        kinetic = kinetic.reshape(GROUP, NC)
        gradient = kinetic + potential[None, :] * values - energy[:, None] * values
        updated = values - 0.3 * gradient / (1.0 - energy)[:, None]
        inside = (block_index[None, :] >= first[:, None]) & (block_index[None, :] < (first + count)[:, None])
        return jnp.where(inside, updated, 0.0).astype(jnp.bfloat16)

    refined = lax.map(refine, (functions.reshape(NG, GROUP, NC), energies.reshape(NG, GROUP),
                               region_start.reshape(NG, GROUP), region_length.reshape(NG, GROUP)))
    identity_block = jnp.concatenate([jnp.eye(GROUP, dtype=jnp.float32)[None],
                                      jnp.zeros((PARTNERS, GROUP, GROUP), jnp.float32)], axis=0)
    weight = 1.0 / (BLOCK * LMAX)

    def correct(group):
        members = jnp.concatenate([group[None].astype(jnp.int32), partner_groups[group].astype(jnp.int32)])
        own_rows = refined[group].astype(jnp.float32)
        blocks = refined[members].astype(jnp.float32)
        intersection = jnp.einsum('gc,khc->kgh', own_rows, blocks, precision=lax.Precision.HIGHEST) * weight
        coupling = (0.5 * (intersection - identity_block)).astype(jnp.bfloat16)
        shifted = jnp.einsum('kgh,khc->gc', coupling.astype(jnp.float32), blocks, precision=lax.Precision.HIGHEST)
        return (own_rows - shifted).astype(jnp.bfloat16)

    corrected = lax.map(correct, jnp.arange(NG, dtype=jnp.int32))
    return corrected.reshape(NF, NC)
```

```python
import functools

import jax
import jax.numpy as jnp
from jax import lax
from jax.experimental import pallas as pl
from jax.experimental.pallas import tpu as pltpu
from jax.sharding import PartitionSpec as P

MESH = pl.DeviceIdType.MESH
SIDE = 32
NC = 32768
BLOCK = 64
GROUP = 64
TAPS = 16
LMAX = 384
FOLD = 384
Z, X, Y = 0, 1, 2
ORDERS = ((Z, X, Y), (X, Y, Z), (Y, Z, X))
F32 = jnp.float32
BF16 = jnp.bfloat16


def position():
    grid = lax.axis_index("grid")
    rep = lax.axis_index("rep")
    return [lax.div(grid, 8), lax.rem(lax.div(grid, 2), 4), rep], lax.rem(grid, 2)


def device_of(pos, core):
    return (pos[Z] * 8 + pos[X] * 2 + core, pos[Y])


def moved(pos, axis, step):
    out = list(pos)
    out[axis] = lax.rem(pos[axis] + step, 4)
    return out


def enter(pos, core):
    barrier = pltpu.get_barrier_semaphore()
    other = 1 - core
    peers = [device_of(pos, other)]
    for axis in (Z, X, Y):
        for step in (1, 2, 3):
            for c in (core, other):
                peers.append(device_of(moved(pos, axis, step), c))
    for peer in peers:
        pl.semaphore_signal(barrier, inc=1, device_id=peer, device_id_type=MESH)
    pl.semaphore_wait(barrier, len(peers))


def remote(src, dst, sems, index, device):
    return pltpu.make_async_remote_copy(
        src_ref=src,
        dst_ref=dst,
        send_sem=sems[0].at[index],
        recv_sem=sems[1].at[index],
        device_id=device,
        device_id_type=MESH,
    )


def stage_one(order, pos, core, src, dst, sems, base):
    axis = order[0]
    mine = pos[axis]
    copies = []
    for step in (1, 3, 2, 0):
        for flip in (0, 1):
            c = core if flip == 0 else 1 - core
            to = moved(pos, axis, step)
            index = base + step * 2 + flip
            if step == 0 and flip == 0:
                copies.append(
                    pltpu.make_async_copy(src.at[mine, core], dst.at[mine, core], sems[1].at[index])
                )
            else:
                copies.append(
                    remote(src.at[to[axis], c], dst.at[mine, core], sems, index, device_of(to, c))
                )
    for copy in copies:
        copy.start()
    return copies


def stage_two(order, pos, core, src, dst, sems, base):
    axis = order[1]
    mine = pos[axis]
    copies = []
    for step in (1, 3, 2, 0):
        to = moved(pos, axis, step)
        index = base + 8 + step
        if step == 0:
            copies.append(pltpu.make_async_copy(src.at[:, :, mine], dst.at[mine], sems[1].at[index]))
        else:
            copies.append(
                remote(src.at[:, :, to[axis]], dst.at[mine], sems, index, device_of(to, core))
            )
    for copy in copies:
        copy.start()
    return copies


def stage_three(order, pos, core, src, dst, sems, base):
    axis = order[2]
    mine = pos[axis]
    copies = []
    for step in (1, 3, 2, 0):
        to = moved(pos, axis, step)
        index = base + 12 + step
        if step == 0:
            copies.append(
                pltpu.make_async_copy(src.at[:, :, :, mine], dst.at[mine], sems[1].at[index])
            )
        else:
            copies.append(
                remote(src.at[:, :, :, to[axis]], dst.at[mine], sems, index, device_of(to, core))
            )
    for copy in copies:
        copy.start()
    return copies


def wait_all(copies):
    for copy in copies:
        copy.wait()


def place(order, z, x, y):
    pos = (z, x, y)
    return pos[order[0]], pos[order[1]], pos[order[2]]


def tap_of(distance, taps_ref):
    out = jnp.zeros(distance.shape, F32)
    for t in range(TAPS):
        out = jnp.where(distance == t, taps_ref[t], out)
    return out


def build_matrices(taps_ref, line_ref, plane_ref):
    rows = lax.broadcasted_iota(jnp.int32, (256, 256), 0)
    cols = lax.broadcasted_iota(jnp.int32, (256, 256), 1)
    same = (rows & 15) == (cols & 15)
    for shift in (-1, 0, 1):
        value = tap_of((cols >> 4) - (rows >> 4) + 16 * shift + TAPS // 2, taps_ref)
        value = jnp.where(same, value, 0.0).astype(BF16)
        if shift == 0:
            line_ref[0:256, 0:256] = value
            line_ref[256:512, 256:512] = value
        elif shift == 1:
            line_ref[0:256, 256:512] = value
        else:
            line_ref[256:512, 0:256] = value
    for shift in (-1, 0, 1):
        value = tap_of((rows >> 5) - (cols >> 5) + 8 * shift + TAPS // 2, taps_ref)
        value = jnp.where((rows & 31) == (cols & 31), value, 0.0)
        if shift == 0:
            inner = tap_of((rows & 31) - (cols & 31) + TAPS // 2, taps_ref)
            value = value + jnp.where((rows >> 5) == (cols >> 5), inner, 0.0)
        value = value.astype(BF16)
        nothing = jnp.zeros_like(value)
        for c in range(4):
            inside = 0 <= c + shift < 4
            plane_ref[c, (shift + 1) * 256 : (shift + 2) * 256, :] = value if inside else nothing


def refine_half(fh, cc, refs):
    fn_ref, params_ref, pot_ref, line_ref, plane_ref, acc_ref, r_ref, send = refs
    c0 = pl.multiple_of(cc * 256, 256)
    cm = pl.multiple_of(jnp.maximum(cc - 1, 0) * 256, 256)
    cp = pl.multiple_of(jnp.minimum(cc + 1, 3) * 256, 256)

    def stacked(f0, offset):
        return jnp.concatenate(
            [fn_ref[f0 : f0 + 16, pl.ds(pl.multiple_of(x * 1024 + offset, 256), 256)] for x in range(SIDE)],
            axis=0,
        )

    for fl in range(2):
        f0 = fh * 32 + fl * 16
        own = stacked(f0, c0)
        acc = jnp.dot(line_ref[...], own, preferred_element_type=F32)
        acc += jnp.dot(stacked(f0, cm), plane_ref[cc, 0:256, :], preferred_element_type=F32)
        acc += jnp.dot(own, plane_ref[cc, 256:512, :], preferred_element_type=F32)
        acc += jnp.dot(stacked(f0, cp), plane_ref[cc, 512:768, :], preferred_element_type=F32)
        acc_ref[fl] = acc

    lane_block = lax.broadcasted_iota(jnp.int32, (16, 256), 1) >> 6
    column = []
    for fl in range(2):
        f0 = fh * 32 + fl * 16
        energy = jnp.broadcast_to(params_ref[f0 : f0 + 16, 0:1], (16, 256))
        first = jnp.broadcast_to(params_ref[f0 : f0 + 16, 1:2], (16, 256)).astype(jnp.int32)
        last = jnp.broadcast_to(params_ref[f0 : f0 + 16, 2:3], (16, 256)).astype(jnp.int32)
        first = first - lane_block
        last = last - lane_block
        column.append((energy, 0.3 / (1.0 - energy), first, last))

    def refined(x, fl):
        f0 = fh * 32 + fl * 16
        energy, step, first, last = column[fl]
        at = pl.ds(pl.multiple_of(x * 1024 + c0, 256), 256)
        value = fn_ref[f0 : f0 + 16, at].astype(F32)
        kinetic = acc_ref[fl, pl.ds(x * 16, 16), :]
        potential = pot_ref[pl.ds(x, 1), pl.ds(c0, 256)]
        gradient = kinetic + (potential - energy) * value
        value = value - step * gradient
        block = x * 16 + cc * 4
        inside = (first <= block) & (last > block)
        value = jnp.where(inside, value, 0.0)
        r_ref[f0 : f0 + 16, at] = value.astype(BF16)
        return value

    low = lax.broadcasted_iota(jnp.int32, (16, 128), 1) < 64
    for xs in range(16):
        z, x = xs // 4, xs % 4
        for fl in range(2):
            value = refined(xs + 8, fl).astype(BF16)
            for h in range(2):
                a1, a2, a3 = place(ORDERS[fh], z, x, cc)
                send[fh][a1, h, a2, a3, fl * 16 : fl * 16 + 16, :] = value[:, h * 128 : h * 128 + 128]
    for xd in range(8):
        folded = [refined(xd, fl) + refined(xd + 24, fl) for fl in range(2)]
        for h in range(2):
            z, x = xd // 2, (xd % 2) * 2 + h
            a, b = (part[:, h * 128 : h * 128 + 128] for part in folded)
            a1, a2, a3 = place(ORDERS[2], z, x, cc)
            first = jnp.where(low, a, pltpu.roll(b, 64, 1))
            second = jnp.where(low, pltpu.roll(a, 64, 1), b)
            send[2][a1, 0, a2, a3, fh * 16 : fh * 16 + 16, :] = first.astype(BF16)
            send[2][a1, 1, a2, a3, fh * 16 : fh * 16 + 16, :] = second.astype(BF16)


def exchange_in(
    fn_hbm, taps_ref, params_ref, pot_ref, start_ref,
    g0, g1, g2, st_out, r_hbm, own_ref,
    fn_ref, line_ref, plane_ref, acc_ref, r_ref,
    s0, s1, s2, a0, a1, a2, b0, b1, b2, st_a, st_b,
    load_sem, store_sem, send_sem, recv_sem, ssend_sem, srecv_sem,
):
    pos, core = position()
    load = pltpu.make_async_copy(fn_hbm, fn_ref, load_sem)
    load.start()
    enter(pos, core)
    sems = (send_sem, recv_sem)
    ssems = (ssend_sem, srecv_sem)
    send, one, two, out = (s0, s1, s2), (a0, a1, a2), (b0, b1, b2), (g0, g1, g2)

    starts = []
    for step in range(4):
        for flip in range(2):
            c = core if flip == 0 else 1 - core
            index = step * 2 + flip
            dst = st_a.at[pos[Z], core]
            if index == 0:
                starts.append(pltpu.make_async_copy(start_ref, dst, srecv_sem.at[index]))
            else:
                to = device_of(moved(pos, Z, step), c)
                starts.append(remote(start_ref, dst, ssems, index, to))
    for copy in starts:
        copy.start()

    build_matrices(taps_ref, line_ref, plane_ref)
    load.wait()
    refs = (fn_ref, params_ref, pot_ref, line_ref, plane_ref, acc_ref, r_ref, send)
    flying = [None] * 3
    for fh in range(2):
        lax.fori_loop(0, 4, lambda cc, carry: (refine_half(fh, cc, refs), carry)[1], 0)
        flying[fh] = stage_one(ORDERS[fh], pos, core, send[fh], one[fh], sems, fh * 16)
    flying[2] = stage_one(ORDERS[2], pos, core, send[2], one[2], sems, 32)
    store = pltpu.make_async_copy(r_ref, r_hbm, store_sem)
    store.start()

    wait_all(starts)
    starts = []
    for step in range(4):
        dst = st_b.at[pos[X]]
        if step == 0:
            starts.append(pltpu.make_async_copy(st_a, dst, srecv_sem.at[8 + step]))
        else:
            starts.append(remote(st_a, dst, ssems, 8 + step, device_of(moved(pos, X, step), core)))
    for copy in starts:
        copy.start()

    def own_part(i, total):
        rows = r_ref[:, pl.ds(pl.multiple_of(i * 1024, 1024), 1024)]
        return total + lax.dot_general(
            rows, rows, (((1,), (1,)), ((), ())), preferred_element_type=F32
        )

    total = lax.fori_loop(0, NC // 1024, own_part, jnp.zeros((GROUP, GROUP), F32))
    unit = lax.broadcasted_iota(jnp.int32, (GROUP, GROUP), 0) == lax.broadcasted_iota(
        jnp.int32, (GROUP, GROUP), 1
    )
    own = 0.5 * (total * (1.0 / (BLOCK * LMAX)) - jnp.where(unit, 1.0, 0.0))
    own_ref[...] = own.astype(BF16)

    wait_all(starts)
    starts = []
    for step in range(4):
        dst = st_out.at[pos[Y]]
        if step == 0:
            starts.append(pltpu.make_async_copy(st_b, dst, srecv_sem.at[12 + step]))
        else:
            starts.append(remote(st_b, dst, ssems, 12 + step, device_of(moved(pos, Y, step), core)))
    for copy in starts:
        copy.start()

    for t in range(3):
        wait_all(flying[t])
        flying[t] = stage_two(ORDERS[t], pos, core, one[t], two[t], sems, t * 16)
    for t in range(3):
        wait_all(flying[t])
        flying[t] = stage_three(ORDERS[t], pos, core, two[t], out[t], sems, t * 16)
    for t in range(3):
        wait_all(flying[t])
    wait_all(starts)
    store.wait()


def run_exchange_in(functions, filter_taps, potential, energies, region_start, region_length):
    params = jnp.stack(
        [energies, region_start.astype(F32), (region_start + region_length).astype(F32)], axis=1
    )
    starts = jnp.pad(region_start.astype(F32), (0, 64)).reshape(1, 128)
    vmem = pl.BlockSpec(memory_space=pltpu.VMEM)
    anywhere = pl.BlockSpec(memory_space=pltpu.HBM)
    piece = jax.ShapeDtypeStruct((4, 4, 4, 2, 32, 128), BF16)
    return pl.pallas_call(
        exchange_in,
        out_shape=(
            piece, piece, piece,
            jax.ShapeDtypeStruct((4, 4, 4, 2, 1, 128), F32),
            jax.ShapeDtypeStruct((GROUP, NC), BF16),
            jax.ShapeDtypeStruct((GROUP, GROUP), BF16),
        ),
        in_specs=[anywhere, pl.BlockSpec(memory_space=pltpu.SMEM), vmem, vmem, vmem],
        out_specs=(anywhere, anywhere, anywhere, anywhere, anywhere, vmem),
        scratch_shapes=[
            pltpu.VMEM((GROUP, NC), BF16),
            pltpu.VMEM((512, 512), BF16),
            pltpu.VMEM((4, 768, 256), BF16),
            pltpu.VMEM((2, 512, 256), F32),
            pltpu.VMEM((GROUP, NC), BF16),
        ]
        + [pltpu.VMEM((4, 2, 4, 4, 32, 128), BF16)] * 3
        + [pltpu.VMEM((4, 2, 4, 4, 32, 128), BF16)] * 3
        + [pltpu.VMEM((4, 4, 2, 4, 32, 128), BF16)] * 3
        + [
            pltpu.VMEM((4, 2, 1, 128), F32),
            pltpu.VMEM((4, 4, 2, 1, 128), F32),
            pltpu.SemaphoreType.DMA,
            pltpu.SemaphoreType.DMA,
            pltpu.SemaphoreType.DMA((48,)),
            pltpu.SemaphoreType.DMA((48,)),
            pltpu.SemaphoreType.DMA((16,)),
            pltpu.SemaphoreType.DMA((16,)),
        ],
        compiler_params=pltpu.CompilerParams(
            collective_id=0, has_side_effects=True, vmem_limit_bytes=60 * 1024 * 1024
        ),
    )(
        functions,
        filter_taps.astype(F32),
        params,
        potential.reshape(SIDE, SIDE * SIDE),
        starts,
    )


def unpack_halves(piece):
    low = lax.broadcasted_iota(jnp.int32, (16, 128), 1) < 64
    parts = []
    for fh in range(2):
        p = piece[fh * 16 : fh * 16 + 16].astype(F32)
        q = pltpu.roll(p, 64, 1)
        parts.append(jnp.where(low, p, q))
        parts.append(jnp.where(low, q, p))
    return jnp.concatenate(parts, axis=0)


def split(g):
    return g >> 5, (g >> 3) & 3, (g >> 2) & 1, g & 3


def orthonormalize(
    partners_ref, g0_hbm, g1_hbm, g2_hbm, st_hbm,
    f0_hbm, f1_hbm, f2_hbm,
    g0, g1, g2, st_ref, rows_ref, after_ref, u_ref,
    q0, q1, q2, p0, p1, p2, m0, m1, m2, t0, t1, t2, n0, n1, n2, v0, v1, v2,
    k0, k1, k2, l0, l1, l2, c0, c1, c2,
    s0, s1, s2, a0, a1, a2, b0, b1, b2,
    load_sem, r_send, r_recv, g_send, g_recv, x_send, x_recv, o_send, o_recv,
):
    pos, core = position()
    loads = [
        pltpu.make_async_copy(src, dst, load_sem.at[i])
        for i, (src, dst) in enumerate(((g0_hbm, g0), (g1_hbm, g1), (g2_hbm, g2), (st_hbm, st_ref)))
    ]
    for copy in loads:
        copy.start()
    enter(pos, core)
    wait_all(loads)
    orders = ORDERS

    for i in range(128):
        y, x, z, c = i >> 5, (i >> 3) & 3, (i >> 1) & 3, i & 1
        rows_ref[z * 32 + x * 8 + c * 4 + y : z * 32 + x * 8 + c * 4 + y + 1, :] = st_ref[y, x, z, c]
    block = (pos[Z] * 2 + lax.div(pos[X], 2)) * 16 + pos[Y] * 4 + lax.rem(pos[X], 2) * 2 + core
    above = jnp.where(rows_ref[...] > block.astype(F32), 1.0, 0.0)
    after_ref[...] = jnp.transpose(above)[0:GROUP]

    lower = lax.broadcasted_iota(jnp.int32, (GROUP, 128), 1) < 64

    def unfold(g, carry):
        z, x, c, y = split(g)
        u_ref[g, 0:32, 0:128] = g0[y, x, z, c]
        u_ref[g, 32:64, 0:128] = g1[z, y, x, c]
        folded = unpack_halves(g2[x, z, y, c])
        turned = pltpu.roll(after_ref[...], lax.rem(128 - g, 128), 1)
        upper = jnp.broadcast_to(turned[:, 0:1], (GROUP, 128)) > 0.5
        keep = jnp.logical_xor(upper, lower)
        u_ref[g, :, 128:256] = jnp.where(keep, folded, 0.0).astype(BF16)
        return carry

    lax.fori_loop(0, 128, unfold, 0, unroll=2)

    q, p, m = (q0, q1, q2), (p0, p1, p2), (m0, m1, m2)
    t, n, v = (t0, t1, t2), (n0, n1, n2), (v0, v1, v2)
    half_low = lax.broadcasted_iota(jnp.int32, (32, 128), 1) < 64

    def intersect(g, carry):
        z, x, c, y = split(g)
        rows = u_ref[g]
        others = jnp.concatenate([u_ref[partners_ref[g, k]] for k in range(3)], axis=0)
        part = lax.dot_general(rows, others, (((1,), (1,)), ((), ())), preferred_element_type=F32)
        q0[z, c, x, y] = part[0:32, 0:128].astype(BF16)
        q1[x, c, y, z] = part[32:64, 0:128].astype(BF16)
        last = jnp.concatenate([part[:, 128:192], part[:, 128:192]], axis=1)
        q2[y, c, z, x] = jnp.where(half_low, last[0:32], last[32:64]).astype(BF16)
        return carry

    lax.fori_loop(0, 128, intersect, 0, unroll=2)

    flying = [None] * 3
    for i in range(3):
        axis = orders[i][0]
        copies = []
        for step in range(4):
            for flip in range(2):
                if step == 0 and flip == 0:
                    continue
                cc = core if flip == 0 else 1 - core
                to = moved(pos, axis, step)
                index = step * 2 + flip
                copies.append(
                    remote(q[i].at[to[axis], cc], p[i].at[index - 1], (r_send, r_recv), i * 16 + index, device_of(to, cc))
                )
        for copy in copies:
            copy.start()
        flying[i] = copies
    for i in range(3):
        wait_all(flying[i])
        mine = pos[orders[i][0]]
        for j in range(4):
            total = q[i][mine, core, j].astype(F32)
            for k in range(7):
                total += p[i][k, j].astype(F32)
            m[i][j] = total.astype(BF16)
        axis = orders[i][1]
        copies = []
        for step in range(1, 4):
            to = moved(pos, axis, step)
            copies.append(
                remote(m[i].at[to[axis]], t[i].at[step - 1], (r_send, r_recv), i * 16 + 8 + step, device_of(to, core))
            )
        for copy in copies:
            copy.start()
        flying[i] = copies
    for i in range(3):
        wait_all(flying[i])
        total = m[i][pos[orders[i][1]]].astype(F32)
        for k in range(3):
            total += t[i][k].astype(F32)
        n[i][...] = total.astype(BF16)
        axis = orders[i][2]
        copies = []
        for step in range(1, 4):
            to = moved(pos, axis, step)
            copies.append(
                remote(n[i].at[to[axis]], v[i].at[step - 1], (r_send, r_recv), i * 16 + 12 + step, device_of(to, core))
            )
        for copy in copies:
            copy.start()
        flying[i] = copies

    kk, ll, cp = (k0, k1, k2), (l0, l1, l2), (c0, c1, c2)
    for i in range(3):
        wait_all(flying[i])
        mine = pos[orders[i][2]]
        total = n[i][mine].astype(F32)
        for k in range(3):
            total += v[i][k].astype(F32)
        kk[i][mine] = (0.5 * (total * (1.0 / (BLOCK * LMAX)))).astype(BF16)
        axis = orders[i][2]
        copies = [
            remote(kk[i].at[mine], kk[i].at[mine], (g_send, g_recv), i * 16 + step, device_of(moved(pos, axis, step), core))
            for step in range(1, 4)
        ]
        for copy in copies:
            copy.start()
        flying[i] = copies
    for i in range(3):
        wait_all(flying[i])
        axis = orders[i][1]
        mine = pos[axis]
        copies = [pltpu.make_async_copy(kk[i], ll[i].at[mine], g_recv.at[i * 16 + 4])]
        for step in range(1, 4):
            copies.append(
                remote(kk[i], ll[i].at[mine], (g_send, g_recv), i * 16 + 4 + step, device_of(moved(pos, axis, step), core))
            )
        for copy in copies:
            copy.start()
        flying[i] = copies
    for i in range(3):
        wait_all(flying[i])
        axis = orders[i][0]
        mine = pos[axis]
        copies = [pltpu.make_async_copy(ll[i], cp[i].at[mine, core], g_recv.at[i * 16 + 8])]
        for step in range(1, 4):
            copies.append(
                remote(ll[i], cp[i].at[mine, core], (g_send, g_recv), i * 16 + 8 + step, device_of(moved(pos, axis, step), core))
            )
        for copy in copies:
            copy.start()
        flying[i] = copies
    passed = []
    for i in range(3):
        axis = orders[i][0]
        for step in range(4):
            flying[i][step].wait()
            at = lax.rem(pos[axis] + 4 - step, 4)
            copy = remote(cp[i].at[at, core], cp[i].at[at, core], (x_send, x_recv), i * 4 + step, device_of(pos, 1 - core))
            copy.start()
            passed.append(copy)
    wait_all(passed)

    s = (s0, s1, s2)

    def shift(g, carry):
        z, x, c, y = split(g)
        others = jnp.concatenate([u_ref[partners_ref[g, k]] for k in range(3)], axis=0)
        third = c2[y, c, z, x]
        third = jnp.concatenate([third[:, 0:64], third[:, 64:128]], axis=0)
        pair = jnp.concatenate([c0[z, c, x, y], c1[x, c, y, z]], axis=0)
        weights = jnp.concatenate([pair, third], axis=1)
        moved_by = jnp.dot(weights, others, preferred_element_type=F32).astype(BF16)
        s0[z, c, x, y] = moved_by[0:48, 0:128]
        s1[x, c, y, z] = moved_by[0:48, 128:256]
        s2[y, c, z, x, 0:16] = moved_by[48:64, 0:128]
        s2[y, c, z, x, 16:32] = moved_by[48:64, 128:256]
        return carry

    lax.fori_loop(0, 128, shift, 0, unroll=2)

    one, two, out = (a0, a1, a2), (b0, b1, b2), (f0_hbm, f1_hbm, f2_hbm)
    sems = (o_send, o_recv)
    for i in range(3):
        flying[i] = stage_one(orders[i], pos, core, s[i], one[i], sems, i * 16)
    for i in range(3):
        wait_all(flying[i])
        flying[i] = stage_two(orders[i], pos, core, one[i], two[i], sems, i * 16)
    for i in range(3):
        wait_all(flying[i])
        flying[i] = stage_three(orders[i], pos, core, two[i], out[i], sems, i * 16)
    for i in range(3):
        wait_all(flying[i])


ROWS = (48, 48, 32)


def run_orthonormalize(partner_groups, g0, g1, g2, starts):
    anywhere = pl.BlockSpec(memory_space=pltpu.HBM)
    dma = pltpu.SemaphoreType.DMA

    def vmem(*shape):
        return pltpu.VMEM(shape, BF16)

    return pl.pallas_call(
        orthonormalize,
        out_shape=tuple(jax.ShapeDtypeStruct((4, 4, 4, 2, r, 128), BF16) for r in ROWS),
        in_specs=[pl.BlockSpec(memory_space=pltpu.SMEM)] + [anywhere] * 4,
        out_specs=(anywhere,) * 3,
        scratch_shapes=[vmem(4, 4, 4, 2, 32, 128)] * 3
        + [pltpu.VMEM((4, 4, 4, 2, 1, 128), F32), pltpu.VMEM((128, 128), F32), pltpu.VMEM((GROUP, 128), F32)]
        + [vmem(128, GROUP, 256)]
        + [vmem(4, 2, 4, 4, 32, 128)] * 3
        + [vmem(7, 4, 4, 32, 128)] * 3
        + [vmem(4, 4, 32, 128)] * 3
        + [vmem(3, 4, 32, 128)] * 3
        + [vmem(4, 32, 128)] * 3
        + [vmem(3, 32, 128)] * 3
        + [vmem(4, 32, 128)] * 3
        + [vmem(4, 4, 32, 128)] * 3
        + [vmem(4, 2, 4, 4, 32, 128)] * 3
        + [vmem(4, 2, 4, 4, r, 128) for r in ROWS]
        + [vmem(4, 2, 4, 4, r, 128) for r in ROWS]
        + [vmem(4, 4, 2, 4, r, 128) for r in ROWS]
        + [dma((4,)), dma((48,)), dma((48,)), dma((48,)), dma((48,)), dma((12,)), dma((12,)), dma((48,)), dma((48,))],
        compiler_params=pltpu.CompilerParams(
            collective_id=1, has_side_effects=True, vmem_limit_bytes=60 * 1024 * 1024
        ),
    )(partner_groups, g0, g1, g2, starts)


def finish(own_ref, r_hbm, f0_hbm, f1_hbm, f2_hbm, o_hbm, r_ref, f0_ref, f1_ref, f2_ref, o_ref, in_sem, out_sem):
    weights = own_ref[...]
    low = lax.broadcasted_iota(jnp.int32, (GROUP, 128), 1) < 64

    def loads(i):
        z, x = lax.div(i, 2), lax.rem(i, 2) * 2
        pairs = []
        for k, (slab, count) in enumerate(((i, 1), (i + 24, 1), (8 + 2 * i, 2))):
            cut = pl.ds(pl.multiple_of(slab * 1024, 1024), count * 1024)
            pairs.append((r_hbm.at[:, cut], r_ref.at[:, cut]))
        cut = pl.ds(x, 2)
        pairs.append((f0_hbm.at[:, cut, z], f0_ref.at[:, cut, z]))
        pairs.append((f1_hbm.at[z, :, cut], f1_ref.at[z, :, cut]))
        pairs.append((f2_hbm.at[cut, z], f2_ref.at[cut, z]))
        return [pltpu.make_async_copy(a, b, in_sem.at[i, k]) for k, (a, b) in enumerate(pairs)]

    def stores(i):
        out = []
        for k, (slab, count) in enumerate(((i, 1), (i + 24, 1), (8 + 2 * i, 2))):
            cut = pl.ds(pl.multiple_of(slab * 1024, 1024), count * 1024)
            out.append(pltpu.make_async_copy(o_ref.at[:, cut], o_hbm.at[:, cut], out_sem.at[i, k]))
        return out

    def each(make):
        def body(i, carry):
            for copy in make(i):
                copy.start()
            return carry

        return body

    lax.fori_loop(0, 8, each(loads), 0)

    def slab_part(slab, y, h, moved_by):
        at = pl.ds(pl.multiple_of(slab * 1024 + y * 256 + h * 128, 128), 128)
        rows = r_ref[:, at]
        shifted = jnp.dot(weights, rows, preferred_element_type=F32)
        o_ref[:, at] = (rows.astype(F32) - shifted - moved_by).astype(BF16)

    def step(i, carry):
        for copy in loads(i):
            copy.wait()
        z, x0 = lax.div(i, 2), lax.rem(i, 2) * 2
        for dx in range(2):
            x = x0 + dx
            for y in range(4):
                twos = []
                for c in range(2):
                    tail = f2_ref[x, z, y, c].astype(F32)
                    single = jnp.concatenate([f0_ref[y, x, z, c].astype(F32), tail[0:16]], axis=0)
                    slab_part(8 + 2 * i + dx, y, c, single)
                    twos.append(jnp.concatenate([f1_ref[z, y, x, c].astype(F32), tail[16:32]], axis=0))
                slab_part(i, y, dx, jnp.where(low, twos[0], pltpu.roll(twos[1], 64, 1)))
                slab_part(i + 24, y, dx, jnp.where(low, pltpu.roll(twos[0], 64, 1), twos[1]))
        for copy in stores(i):
            copy.start()
        return carry

    lax.fori_loop(0, 8, step, 0)

    def last(i, carry):
        for copy in stores(i):
            copy.wait()
        return carry

    lax.fori_loop(0, 8, last, 0)


def run_finish(own, refined, f0, f1, f2):
    anywhere = pl.BlockSpec(memory_space=pltpu.HBM)
    return pl.pallas_call(
        finish,
        out_shape=jax.ShapeDtypeStruct((GROUP, NC), BF16),
        in_specs=[pl.BlockSpec(memory_space=pltpu.VMEM)] + [anywhere] * 4,
        out_specs=anywhere,
        scratch_shapes=[pltpu.VMEM((GROUP, NC), BF16)]
        + [pltpu.VMEM((4, 4, 4, 2, r, 128), BF16) for r in ROWS]
        + [pltpu.VMEM((GROUP, NC), BF16), pltpu.SemaphoreType.DMA((8, 6)), pltpu.SemaphoreType.DMA((8, 3))],
        compiler_params=pltpu.CompilerParams(vmem_limit_bytes=40 * 1024 * 1024),
    )(own, refined, f0, f1, f2)


def on_device(functions, filter_taps, potential, energies, region_start, region_length, partner_groups):
    g0, g1, g2, starts, refined, own = run_exchange_in(
        functions, filter_taps, potential, energies, region_start, region_length
    )
    f0, f1, f2 = run_orthonormalize(partner_groups, g0, g1, g2, starts)
    return run_finish(own, refined, f0, f1, f2)


def solution(mesh):
    return jax.shard_map(
        on_device,
        mesh=mesh,
        in_specs=(
            P(("grid", "rep"), None),
            P(),
            P(),
            P(("grid", "rep")),
            P(("grid", "rep")),
            P(("grid", "rep")),
            P(),
        ),
        out_specs=P(("grid", "rep"), None),
        check_vma=False,
    )
```

```python
import functools

import jax
import jax.numpy as jnp
from jax import lax
from jax.experimental import pallas as pl
from jax.experimental.pallas import tpu as pltpu
from jax.sharding import PartitionSpec as P

MESH = pl.DeviceIdType.MESH
SIDE = 32
NC = 32768
BLOCK = 64
GROUP = 64
TAPS = 16
LMAX = 384
FOLD = 384
Z, X, Y = 0, 1, 2
ORDERS = ((Z, X, Y), (X, Y, Z), (Y, Z, X))
F32 = jnp.float32
BF16 = jnp.bfloat16


def position():
    grid = lax.axis_index("grid")
    rep = lax.axis_index("rep")
    return [lax.div(grid, 8), lax.rem(lax.div(grid, 2), 4), rep], lax.rem(grid, 2)


def device_of(pos, core):
    return (pos[Z] * 8 + pos[X] * 2 + core, pos[Y])


def moved(pos, axis, step):
    out = list(pos)
    out[axis] = lax.rem(pos[axis] + step, 4)
    return out


def enter(pos, core):
    barrier = pltpu.get_barrier_semaphore()
    other = 1 - core
    peers = [device_of(pos, other)]
    for axis in (Z, X, Y):
        for step in (1, 2, 3):
            for c in (core, other):
                peers.append(device_of(moved(pos, axis, step), c))
    for peer in peers:
        pl.semaphore_signal(barrier, inc=1, device_id=peer, device_id_type=MESH)
    pl.semaphore_wait(barrier, len(peers))


def remote(src, dst, sems, index, device):
    return pltpu.make_async_remote_copy(
        src_ref=src,
        dst_ref=dst,
        send_sem=sems[0].at[index],
        recv_sem=sems[1].at[index],
        device_id=device,
        device_id_type=MESH,
    )


def part_of(pos, i):
    return lax.rem(pos[Y] + 1 + i, 4)


def stage_one(t, pos, core, src, dst, sems, i):
    axis = ORDERS[t][0]
    mine = pos[axis]
    yy = part_of(pos, i)
    remotes, local = [], None
    for step in (1, 3, 2, 0):
        for flip in (0, 1):
            c = core if flip == 0 else 1 - core
            to = moved(pos, axis, step)
            index = t * 40 + i * 8 + step * 2 + flip
            if t == 0:
                a, b = src.at[to[axis], c, :, yy], dst.at[mine, core, :, yy]
            else:
                a, b = src.at[to[axis], c, yy], dst.at[mine, core, yy]
            if step == 0 and flip == 0:
                local = pltpu.make_async_copy(a, b, sems[1].at[index])
            else:
                remotes.append(remote(a, b, sems, index, device_of(to, c)))
    return remotes + [local]


def stage_one_y(pos, core, src, dst, sems, step, flips=(0, 1)):
    mine = pos[Y]
    to = moved(pos, Y, step)
    out = []
    for flip in flips:
        c = core if flip == 0 else 1 - core
        out.append(
            remote(src.at[to[Y], c], dst.at[mine, core], sems, 80 + step * 2 + flip, device_of(to, c))
        )
    return out


def keep_y(pos, core, src, dst, sems):
    return pltpu.make_async_copy(src.at[pos[Y], core], dst.at[pos[Y], core], sems[1].at[80])


def start_part(pos, core, src, dst, sems, i):
    for t in (0, 1):
        for copy in stage_one(t, pos, core, src[t], dst[t], sems, i):
            copy.start()

    @pl.when(i < 3)
    def _():
        for copy in stage_one_y(pos, core, src[2], dst[2], sems, i + 1):
            copy.start()

    @pl.when(i == 3)
    def _():
        stage_one_y(pos, core, src[2], dst[2], sems, 0, (1,))[0].start()
        keep_y(pos, core, src[2], dst[2], sems).start()


def wait_one(t, pos, core, src, dst, sems):
    if t < 2:
        def body(i, carry):
            wait_all(stage_one(t, pos, core, src[t], dst[t], sems, i))
            return carry

        lax.fori_loop(0, 4, body, 0)
    else:
        for step in range(1, 4):
            wait_all(stage_one_y(pos, core, src[2], dst[2], sems, step))
        stage_one_y(pos, core, src[2], dst[2], sems, 0, (1,))[0].wait()
        keep_y(pos, core, src[2], dst[2], sems).wait()


def stage_two(t, pos, core, src, dst, sems):
    axis = ORDERS[t][1]
    mine = pos[axis]
    copies = []
    for step in (1, 3, 2, 0):
        to = moved(pos, axis, step)
        index = 120 + t * 8 + step
        if step == 0:
            copies.append(pltpu.make_async_copy(src.at[:, :, mine], dst.at[mine], sems[1].at[index]))
        else:
            copies.append(remote(src.at[:, :, to[axis]], dst.at[mine], sems, index, device_of(to, core)))
    for copy in copies:
        copy.start()
    return copies


def stage_three(t, pos, core, src, dst, sems):
    axis = ORDERS[t][2]
    mine = pos[axis]
    copies = []
    for step in (1, 3, 2, 0):
        to = moved(pos, axis, step)
        index = 120 + t * 8 + 4 + step
        if step == 0:
            copies.append(pltpu.make_async_copy(src.at[:, :, :, mine], dst.at[mine], sems[1].at[index]))
        else:
            copies.append(
                remote(src.at[:, :, :, to[axis]], dst.at[mine], sems, index, device_of(to, core))
            )
    for copy in copies:
        copy.start()
    return copies


SEMS = 144


def wait_all(copies):
    for copy in copies:
        copy.wait()


def place(order, z, x, y):
    pos = (z, x, y)
    return pos[order[0]], pos[order[1]], pos[order[2]]


def tap_of(distance, taps_ref):
    taps = taps_ref[...].astype(F32)
    out = jnp.zeros(distance.shape, F32)
    for t in range(TAPS):
        out = jnp.where(distance == t, jnp.broadcast_to(taps[:, t : t + 1], distance.shape), out)
    return out


def build_matrices(taps_ref, line_ref, plane_ref):
    rows = lax.broadcasted_iota(jnp.int32, (256, 256), 0)
    cols = lax.broadcasted_iota(jnp.int32, (256, 256), 1)
    same = (rows & 15) == (cols & 15)
    for shift in (-1, 0, 1):
        value = tap_of((cols >> 4) - (rows >> 4) + 16 * shift + TAPS // 2, taps_ref)
        value = jnp.where(same, value, 0.0).astype(BF16)
        if shift == 0:
            line_ref[0:256, 0:256] = value
            line_ref[256:512, 256:512] = value
        elif shift == 1:
            line_ref[0:256, 256:512] = value
        else:
            line_ref[256:512, 0:256] = value
    for shift in (-1, 0, 1):
        value = tap_of((rows >> 5) - (cols >> 5) + 8 * shift + TAPS // 2, taps_ref)
        value = jnp.where((rows & 31) == (cols & 31), value, 0.0)
        if shift == 0:
            inner = tap_of((rows & 31) - (cols & 31) + TAPS // 2, taps_ref)
            value = value + jnp.where((rows >> 5) == (cols >> 5), inner, 0.0)
        value = value.astype(BF16)
        nothing = jnp.zeros_like(value)
        for c in range(4):
            inside = 0 <= c + shift < 4
            plane_ref[c, (shift + 1) * 256 : (shift + 2) * 256, :] = value if inside else nothing


def refine_half(fh, cc, refs):
    fn_ref, params_ref, pot_ref, line_ref, plane_ref, acc_ref, r_ref, send = refs
    c0 = pl.multiple_of(cc * 256, 256)
    cm = pl.multiple_of(jnp.maximum(cc - 1, 0) * 256, 256)
    cp = pl.multiple_of(jnp.minimum(cc + 1, 3) * 256, 256)

    def stacked(f0, offset):
        return jnp.concatenate(
            [fn_ref[f0 : f0 + 16, pl.ds(pl.multiple_of(x * 1024 + offset, 256), 256)] for x in range(SIDE)],
            axis=0,
        )

    for fl in range(2):
        f0 = fh * 32 + fl * 16
        own = stacked(f0, c0)
        acc = jnp.dot(line_ref[...], own, preferred_element_type=F32)
        acc += jnp.dot(stacked(f0, cm), plane_ref[cc, 0:256, :], preferred_element_type=F32)
        acc += jnp.dot(own, plane_ref[cc, 256:512, :], preferred_element_type=F32)
        acc += jnp.dot(stacked(f0, cp), plane_ref[cc, 512:768, :], preferred_element_type=F32)
        acc_ref[fl] = acc

    lane_block = lax.broadcasted_iota(jnp.int32, (16, 256), 1) >> 6
    column = []
    for fl in range(2):
        f0 = fh * 32 + fl * 16
        energy = jnp.broadcast_to(params_ref[f0 : f0 + 16, 0:1], (16, 256))
        first = jnp.broadcast_to(params_ref[f0 : f0 + 16, 1:2], (16, 256)).astype(jnp.int32)
        last = jnp.broadcast_to(params_ref[f0 : f0 + 16, 2:3], (16, 256)).astype(jnp.int32)
        first = first - lane_block
        last = last - lane_block
        column.append((energy, 0.3 / (1.0 - energy), first, last))

    def refined(x, fl):
        f0 = fh * 32 + fl * 16
        energy, step, first, last = column[fl]
        at = pl.ds(pl.multiple_of(x * 1024 + c0, 256), 256)
        value = fn_ref[f0 : f0 + 16, at].astype(F32)
        kinetic = acc_ref[fl, pl.ds(x * 16, 16), :]
        row = x * 8 + cc * 2
        potential = jnp.concatenate([pot_ref[pl.ds(row, 1), :], pot_ref[pl.ds(row + 1, 1), :]], axis=1)
        gradient = kinetic + (potential - energy) * value
        value = value - step * gradient
        block = x * 16 + cc * 4
        inside = (first <= block) & (last > block)
        value = jnp.where(inside, value, 0.0)
        r_ref[f0 : f0 + 16, at] = value.astype(BF16)
        return value

    low = lax.broadcasted_iota(jnp.int32, (16, 128), 1) < 64
    for xs in range(16):
        z, x = xs // 4, xs % 4
        for fl in range(2):
            value = refined(xs + 8, fl).astype(BF16)
            for h in range(2):
                a1, a2, a3 = place(ORDERS[fh], z, x, cc)
                send[fh][a1, h, a2, a3, fl * 16 : fl * 16 + 16, :] = value[:, h * 128 : h * 128 + 128]
    for xd in range(8):
        folded = [refined(xd, fl) + refined(xd + 24, fl) for fl in range(2)]
        for h in range(2):
            z, x = xd // 2, (xd % 2) * 2 + h
            a, b = (part[:, h * 128 : h * 128 + 128] for part in folded)
            a1, a2, a3 = place(ORDERS[2], z, x, cc)
            first = jnp.where(low, a, pltpu.roll(b, 64, 1))
            second = jnp.where(low, pltpu.roll(a, 64, 1), b)
            send[2][a1, 0, a2, a3, fh * 16 : fh * 16 + 16, :] = first.astype(BF16)
            send[2][a1, 1, a2, a3, fh * 16 : fh * 16 + 16, :] = second.astype(BF16)


def unpack_halves(piece):
    low = lax.broadcasted_iota(jnp.int32, (16, 128), 1) < 64
    parts = []
    for fh in range(2):
        p = piece[fh * 16 : fh * 16 + 16].astype(F32)
        q = pltpu.roll(p, 64, 1)
        parts.append(jnp.where(low, p, q))
        parts.append(jnp.where(low, q, p))
    return jnp.concatenate(parts, axis=0)


def split(g):
    return g >> 5, (g >> 3) & 3, (g >> 2) & 1, g & 3


def orthonormalize(
    partners_ref, fn_hbm, taps_ref, energy_ref, start_ref, length_ref, pot_ref,
    f0_hbm, f1_hbm, f2_hbm, r_hbm, own_ref,
    fn_ref, line_ref, plane_ref, acc_ref, r_ref, square_ref, params_ref, first_ref,
    e0, e1, e2, a0, a1, a2, b0, b1, b2, g0, g1, g2, st_a, st_b, st_c,
    after_ref, u_ref,
    q0, q1, q2, p0, p1, p2, m0, m1, m2, t0, t1, t2, n0, n1, n2, v0, v1, v2,
    k0, k1, k2, l0, l1, l2, c0, c1, c2,
    s0, s1, s2, h0, h1, h2, i0, i1, i2,
    load_sem, store_sem, in_send, in_recv, st_send, st_recv, r_send, r_recv, g_send, g_recv, x_send, x_recv,
    o_send, o_recv,
):
    pos, core = position()
    load = pltpu.make_async_copy(fn_hbm, fn_ref, load_sem)
    load.start()
    enter(pos, core)

    first_ref[...] = jnp.zeros((1, 128), F32)
    first_ref[0:1, 0:GROUP] = start_ref[...].astype(F32)
    st_sems = (st_send, st_recv)
    starts = []
    for step in range(4):
        for flip in range(2):
            c = core if flip == 0 else 1 - core
            index = step * 2 + flip
            dst = st_a.at[pos[Z], core]
            if index == 0:
                starts.append(pltpu.make_async_copy(first_ref, dst, st_recv.at[index]))
            else:
                starts.append(remote(first_ref, dst, st_sems, index, device_of(moved(pos, Z, step), c)))

    square_ref[...] = jnp.zeros((128, 128), F32)
    square_ref[0:1, 0:GROUP] = energy_ref[...]
    square_ref[1:2, 0:GROUP] = start_ref[...].astype(F32)
    square_ref[2:3, 0:GROUP] = (start_ref[...] + length_ref[...]).astype(F32)
    params_ref[...] = jnp.transpose(square_ref[...])[0:GROUP]
    build_matrices(taps_ref, line_ref, plane_ref)
    for copy in starts:
        copy.start()
    load.wait()
    send, one, two, got = (e0, e1, e2), (a0, a1, a2), (b0, b1, b2), (g0, g1, g2)
    sems = (in_send, in_recv)
    refs = (fn_ref, params_ref, pot_ref, line_ref, plane_ref, acc_ref, r_ref, send)

    def refine(i, carry):
        for fh in range(2):
            refine_half(fh, part_of(pos, i), refs)
        start_part(pos, core, send, one, sems, i)
        return carry

    lax.fori_loop(0, 4, refine, 0)
    store = pltpu.make_async_copy(r_ref, r_hbm, store_sem)
    store.start()

    wait_all(starts)
    starts = []
    for step in range(4):
        dst = st_b.at[pos[X]]
        if step == 0:
            starts.append(pltpu.make_async_copy(st_a, dst, st_recv.at[8 + step]))
        else:
            starts.append(remote(st_a, dst, st_sems, 8 + step, device_of(moved(pos, X, step), core)))
    for copy in starts:
        copy.start()

    flying = [None] * 3
    for t in range(3):
        wait_one(t, pos, core, send, one, sems)
        flying[t] = stage_two(t, pos, core, one[t], two[t], sems)
    wait_all(starts)
    starts = []
    for step in range(4):
        dst = st_c.at[pos[Y]]
        if step == 0:
            starts.append(pltpu.make_async_copy(st_b, dst, st_recv.at[12 + step]))
        else:
            starts.append(remote(st_b, dst, st_sems, 12 + step, device_of(moved(pos, Y, step), core)))
    for copy in starts:
        copy.start()

    def own_part(i, total):
        rows = r_ref[:, pl.ds(pl.multiple_of(i * 1024, 1024), 1024)]
        return total + lax.dot_general(
            rows, rows, (((1,), (1,)), ((), ())), preferred_element_type=F32
        )

    total = lax.fori_loop(0, NC // 1024, own_part, jnp.zeros((GROUP, GROUP), F32))
    unit = lax.broadcasted_iota(jnp.int32, (GROUP, GROUP), 0) == lax.broadcasted_iota(
        jnp.int32, (GROUP, GROUP), 1
    )
    own = 0.5 * (total * (1.0 / (BLOCK * LMAX)) - jnp.where(unit, 1.0, 0.0))
    own_ref[...] = own.astype(BF16)

    for t in (2, 0, 1):
        wait_all(flying[t])
        flying[t] = stage_three(t, pos, core, two[t], got[t], sems)

    wait_all(starts)
    for i in range(128):
        y, x, z, c = i >> 5, (i >> 3) & 3, (i >> 1) & 3, i & 1
        square_ref[z * 32 + x * 8 + c * 4 + y : z * 32 + x * 8 + c * 4 + y + 1, :] = st_c[y, x, z, c]
    block = (pos[Z] * 2 + lax.div(pos[X], 2)) * 16 + pos[Y] * 4 + lax.rem(pos[X], 2) * 2 + core
    above = jnp.where(square_ref[...] > block.astype(F32), 1.0, 0.0)
    after_ref[...] = jnp.transpose(above)[0:GROUP]

    lower = lax.broadcasted_iota(jnp.int32, (GROUP, 128), 1) < 64

    for k in (3, 0, 1, 2):
        step = (1, 3, 2, 0)[k]
        flying[2][k].wait()
        x = lax.rem(pos[X] + 4 - step, 4)

        def unfold(j, carry, x=x):
            z, y, c = j >> 3, (j >> 1) & 3, j & 1
            g = z * 32 + x * 8 + c * 4 + y
            folded = unpack_halves(g2[x, z, y, c])
            turned = pltpu.roll(after_ref[...], lax.rem(128 - g, 128), 1)
            upper = jnp.broadcast_to(turned[:, 0:1], (GROUP, 128)) > 0.5
            keep = jnp.logical_xor(upper, lower)
            u_ref[g] = jnp.where(keep, folded, 0.0).astype(BF16)
            return carry

        lax.fori_loop(0, 32, unfold, 0, unroll=2)
    wait_all(flying[0])
    wait_all(flying[1])

    def columns(g):
        z, x, c, y = split(g)
        return jnp.concatenate(
            [jnp.concatenate([g0[y, x, z, c], g1[z, y, x, c]], axis=0), u_ref[g]], axis=1
        )

    def partners(g):
        return jnp.concatenate([columns(partners_ref[k, g]) for k in range(3)], axis=0)

    half_low = lax.broadcasted_iota(jnp.int32, (32, 128), 1) < 64
    q, p, m = (q0, q1, q2), (p0, p1, p2), (m0, m1, m2)
    t, n, v = (t0, t1, t2), (n0, n1, n2), (v0, v1, v2)
    sums = (r_send, r_recv)

    def intersect_part(i, carry):
        y = part_of(pos, i)

        def intersect(j, inner):
            z, x, c = j >> 3, (j >> 1) & 3, j & 1
            g = z * 32 + x * 8 + c * 4 + y
            part = lax.dot_general(
                columns(g), partners(g), (((1,), (1,)), ((), ())), preferred_element_type=F32
            )
            q0[z, c, x, y] = part[0:32, 0:128].astype(BF16)
            q1[x, c, y, z] = part[32:64, 0:128].astype(BF16)
            last = jnp.concatenate([part[:, 128:192], part[:, 128:192]], axis=1)
            q2[y, c, z, x] = jnp.where(half_low, last[0:32], last[32:64]).astype(BF16)
            return inner

        lax.fori_loop(0, 32, intersect, 0, unroll=2)
        start_part(pos, core, q, p, sums, i)
        return carry

    lax.fori_loop(0, 4, intersect_part, 0)

    orders = ORDERS
    for i in range(3):
        wait_one(i, pos, core, q, p, sums)
        for j in range(4):
            total = p[i][0, 0, j].astype(F32)
            for k in range(1, 8):
                total += p[i][k >> 1, k & 1, j].astype(F32)
            m[i][j] = total.astype(BF16)
        axis = orders[i][1]
        copies = []
        for step in range(1, 4):
            to = moved(pos, axis, step)
            copies.append(
                remote(m[i].at[to[axis]], t[i].at[step - 1], sums, 120 + i * 8 + step, device_of(to, core))
            )
        for copy in copies:
            copy.start()
        flying[i] = copies
    for i in range(3):
        wait_all(flying[i])
        total = m[i][pos[orders[i][1]]].astype(F32)
        for k in range(3):
            total += t[i][k].astype(F32)
        n[i][...] = total.astype(BF16)
        axis = orders[i][2]
        copies = []
        for step in range(1, 4):
            to = moved(pos, axis, step)
            copies.append(
                remote(n[i].at[to[axis]], v[i].at[step - 1], sums, 120 + i * 8 + 4 + step, device_of(to, core))
            )
        for copy in copies:
            copy.start()
        flying[i] = copies

    kk, ll, cp = (k0, k1, k2), (l0, l1, l2), (c0, c1, c2)
    for i in range(3):
        wait_all(flying[i])
        mine = pos[orders[i][2]]
        total = n[i][mine].astype(F32)
        for k in range(3):
            total += v[i][k].astype(F32)
        kk[i][mine] = (0.5 * (total * (1.0 / (BLOCK * LMAX)))).astype(BF16)
        axis = orders[i][2]
        copies = [
            remote(kk[i].at[mine], kk[i].at[mine], (g_send, g_recv), i * 16 + step, device_of(moved(pos, axis, step), core))
            for step in range(1, 4)
        ]
        for copy in copies:
            copy.start()
        flying[i] = copies
    for i in range(3):
        wait_all(flying[i])
        axis = orders[i][1]
        mine = pos[axis]
        copies = [pltpu.make_async_copy(kk[i], ll[i].at[mine], g_recv.at[i * 16 + 4])]
        for step in range(1, 4):
            copies.append(
                remote(kk[i], ll[i].at[mine], (g_send, g_recv), i * 16 + 4 + step, device_of(moved(pos, axis, step), core))
            )
        for copy in copies:
            copy.start()
        flying[i] = copies
    for i in range(3):
        wait_all(flying[i])
        axis = orders[i][0]
        mine = pos[axis]
        copies = [pltpu.make_async_copy(ll[i], cp[i].at[mine, core], g_recv.at[i * 16 + 8])]
        for step in range(1, 4):
            copies.append(
                remote(ll[i], cp[i].at[mine, core], (g_send, g_recv), i * 16 + 8 + step, device_of(moved(pos, axis, step), core))
            )
        for copy in copies:
            copy.start()
        flying[i] = copies
    passed = []
    for step in (0, 1, 3, 2):
        for i in range(3):
            axis = orders[i][0]
            flying[i][step].wait()
            at = lax.rem(pos[axis] + 4 - step, 4)
            copy = remote(cp[i].at[at, core], cp[i].at[at, core], (x_send, x_recv), i * 4 + step, device_of(pos, 1 - core))
            copy.start()
            passed.append(copy)
    wait_all(passed)

    s, back, turn, out = (s0, s1, s2), (h0, h1, h2), (i0, i1, i2), (f0_hbm, f1_hbm, f2_hbm)
    sems = (o_send, o_recv)

    def shift_part(i, carry):
        y = part_of(pos, i)

        def shift(j, inner):
            z, x, c = j >> 3, (j >> 1) & 3, j & 1
            g = z * 32 + x * 8 + c * 4 + y
            third = c2[y, c, z, x]
            third = jnp.concatenate([third[:, 0:64], third[:, 64:128]], axis=0)
            pair = jnp.concatenate([c0[z, c, x, y], c1[x, c, y, z]], axis=0)
            weights = jnp.concatenate([pair, third], axis=1)
            moved_by = jnp.dot(weights, partners(g), preferred_element_type=F32).astype(BF16)
            s0[z, c, x, y] = moved_by[0:48, 0:128]
            s1[x, c, y, z] = moved_by[0:48, 128:256]
            s2[y, c, z, x, 0:16] = moved_by[48:64, 0:128]
            s2[y, c, z, x, 16:32] = moved_by[48:64, 128:256]
            return inner

        lax.fori_loop(0, 32, shift, 0, unroll=2)
        start_part(pos, core, s, back, sems, i)
        return carry

    lax.fori_loop(0, 4, shift_part, 0)
    for i in range(3):
        wait_one(i, pos, core, s, back, sems)
        flying[i] = stage_two(i, pos, core, back[i], turn[i], sems)
    for i in range(3):
        wait_all(flying[i])
        flying[i] = stage_three(i, pos, core, turn[i], out[i], sems)
    for i in range(3):
        wait_all(flying[i])
    store.wait()


ROWS = (48, 48, 32)


def run_orthonormalize(
    functions, filter_taps, potential, energies, region_start, region_length, partner_groups
):
    anywhere = pl.BlockSpec(memory_space=pltpu.HBM)
    whole = pl.BlockSpec(memory_space=pltpu.VMEM)
    dma = pltpu.SemaphoreType.DMA

    def vmem(*shape, kind=BF16):
        return pltpu.VMEM(shape, kind)

    return pl.pallas_call(
        orthonormalize,
        out_shape=tuple(jax.ShapeDtypeStruct((4, 4, 4, 2, r, 128), BF16) for r in ROWS)
        + (jax.ShapeDtypeStruct((GROUP, NC), BF16), jax.ShapeDtypeStruct((GROUP, GROUP), BF16)),
        in_specs=[pl.BlockSpec(memory_space=pltpu.SMEM), anywhere] + [whole] * 5,
        out_specs=(anywhere,) * 4 + (whole,),
        scratch_shapes=[
            vmem(GROUP, NC),
            vmem(512, 512),
            vmem(4, 768, 256),
            vmem(2, 512, 256, kind=F32),
            vmem(GROUP, NC),
            vmem(128, 128, kind=F32),
            vmem(GROUP, 128, kind=F32),
            vmem(1, 128, kind=F32),
        ]
        + [vmem(4, 2, 4, 4, 32, 128)] * 6
        + [vmem(4, 4, 2, 4, 32, 128)] * 3
        + [vmem(4, 4, 4, 2, 32, 128)] * 3
        + [vmem(4, 2, 1, 128, kind=F32), vmem(4, 4, 2, 1, 128, kind=F32), vmem(4, 4, 4, 2, 1, 128, kind=F32)]
        + [vmem(GROUP, 128, kind=F32), vmem(128, GROUP, 128)]
        + [vmem(4, 2, 4, 4, 32, 128)] * 6
        + [vmem(4, 4, 32, 128)] * 3
        + [vmem(3, 4, 32, 128)] * 3
        + [vmem(4, 32, 128)] * 3
        + [vmem(3, 32, 128)] * 3
        + [vmem(4, 32, 128)] * 3
        + [vmem(4, 4, 32, 128)] * 3
        + [vmem(4, 2, 4, 4, 32, 128)] * 3
        + [vmem(4, 2, 4, 4, r, 128) for r in ROWS]
        + [vmem(4, 2, 4, 4, r, 128) for r in ROWS]
        + [vmem(4, 4, 2, 4, r, 128) for r in ROWS]
        + [dma, dma, dma((SEMS,)), dma((SEMS,)), dma((16,)), dma((16,)), dma((SEMS,)), dma((SEMS,))]
        + [dma((48,)), dma((48,)), dma((12,)), dma((12,)), dma((SEMS,)), dma((SEMS,))],
        compiler_params=pltpu.CompilerParams(
            collective_id=0, has_side_effects=True, vmem_limit_bytes=63 * 1024 * 1024
        ),
    )(
        partner_groups.T,
        functions,
        filter_taps.reshape(1, TAPS),
        energies.reshape(1, GROUP),
        region_start.reshape(1, GROUP),
        region_length.reshape(1, GROUP),
        potential.reshape(256, 128),
    )


def finish(own_ref, r_hbm, f0_hbm, f1_hbm, f2_hbm, o_hbm, r_ref, f0_ref, f1_ref, f2_ref, o_ref, in_sem, out_sem):
    weights = own_ref[...]
    low = lax.broadcasted_iota(jnp.int32, (GROUP, 128), 1) < 64

    def loads(i):
        z, x = lax.div(i, 2), lax.rem(i, 2) * 2
        pairs = []
        for k, (slab, count) in enumerate(((i, 1), (i + 24, 1), (8 + 2 * i, 2))):
            cut = pl.ds(pl.multiple_of(slab * 1024, 1024), count * 1024)
            pairs.append((r_hbm.at[:, cut], r_ref.at[:, cut]))
        cut = pl.ds(x, 2)
        pairs.append((f0_hbm.at[:, cut, z], f0_ref.at[:, cut, z]))
        pairs.append((f1_hbm.at[z, :, cut], f1_ref.at[z, :, cut]))
        pairs.append((f2_hbm.at[cut, z], f2_ref.at[cut, z]))
        return [pltpu.make_async_copy(a, b, in_sem.at[i, k]) for k, (a, b) in enumerate(pairs)]

    def stores(i):
        out = []
        for k, (slab, count) in enumerate(((i, 1), (i + 24, 1), (8 + 2 * i, 2))):
            cut = pl.ds(pl.multiple_of(slab * 1024, 1024), count * 1024)
            out.append(pltpu.make_async_copy(o_ref.at[:, cut], o_hbm.at[:, cut], out_sem.at[i, k]))
        return out

    def each(make):
        def body(i, carry):
            for copy in make(i):
                copy.start()
            return carry

        return body

    lax.fori_loop(0, 8, each(loads), 0)

    def slab_part(slab, y, h, moved_by):
        at = pl.ds(pl.multiple_of(slab * 1024 + y * 256 + h * 128, 128), 128)
        rows = r_ref[:, at]
        shifted = jnp.dot(weights, rows, preferred_element_type=F32)
        o_ref[:, at] = (rows.astype(F32) - shifted - moved_by).astype(BF16)

    def step(i, carry):
        for copy in loads(i):
            copy.wait()
        z, x0 = lax.div(i, 2), lax.rem(i, 2) * 2
        for dx in range(2):
            x = x0 + dx
            for y in range(4):
                twos = []
                for c in range(2):
                    tail = f2_ref[x, z, y, c].astype(F32)
                    single = jnp.concatenate([f0_ref[y, x, z, c].astype(F32), tail[0:16]], axis=0)
                    slab_part(8 + 2 * i + dx, y, c, single)
                    twos.append(jnp.concatenate([f1_ref[z, y, x, c].astype(F32), tail[16:32]], axis=0))
                slab_part(i, y, dx, jnp.where(low, twos[0], pltpu.roll(twos[1], 64, 1)))
                slab_part(i + 24, y, dx, jnp.where(low, pltpu.roll(twos[0], 64, 1), twos[1]))
        for copy in stores(i):
            copy.start()
        return carry

    lax.fori_loop(0, 8, step, 0)

    def last(i, carry):
        for copy in stores(i):
            copy.wait()
        return carry

    lax.fori_loop(0, 8, last, 0)


def run_finish(own, refined, f0, f1, f2):
    anywhere = pl.BlockSpec(memory_space=pltpu.HBM)
    return pl.pallas_call(
        finish,
        out_shape=jax.ShapeDtypeStruct((GROUP, NC), BF16),
        in_specs=[pl.BlockSpec(memory_space=pltpu.VMEM)] + [anywhere] * 4,
        out_specs=anywhere,
        scratch_shapes=[pltpu.VMEM((GROUP, NC), BF16)]
        + [pltpu.VMEM((4, 4, 4, 2, r, 128), BF16) for r in ROWS]
        + [pltpu.VMEM((GROUP, NC), BF16), pltpu.SemaphoreType.DMA((8, 6)), pltpu.SemaphoreType.DMA((8, 3))],
        compiler_params=pltpu.CompilerParams(vmem_limit_bytes=63 * 1024 * 1024),
    )(own, refined, f0, f1, f2)


def on_device(functions, filter_taps, potential, energies, region_start, region_length, partner_groups):
    f0, f1, f2, refined, own = run_orthonormalize(
        functions, filter_taps, potential, energies, region_start, region_length, partner_groups
    )
    return run_finish(own, refined, f0, f1, f2)


def solution(mesh):
    return jax.shard_map(
        on_device,
        mesh=mesh,
        in_specs=(
            P(("grid", "rep"), None),
            P(),
            P(),
            P(("grid", "rep")),
            P(("grid", "rep")),
            P(("grid", "rep")),
            P(),
        ),
        out_specs=P(("grid", "rep"), None),
        check_vma=False,
    )
```

```python
import functools

import jax
import jax.numpy as jnp
from jax import lax
from jax.experimental import pallas as pl
from jax.experimental.pallas import tpu as pltpu
from jax.sharding import PartitionSpec as P

MESH = pl.DeviceIdType.MESH
SIDE = 32
NC = 32768
BLOCK = 64
GROUP = 64
TAPS = 16
LMAX = 384
FOLD = 384
Z, X, Y = 0, 1, 2
ORDERS = ((Z, X, Y), (X, Y, Z), (Y, Z, X))
F32 = jnp.float32
BF16 = jnp.bfloat16


def position():
    grid = lax.axis_index("grid")
    rep = lax.axis_index("rep")
    return [lax.div(grid, 8), lax.rem(lax.div(grid, 2), 4), rep], lax.rem(grid, 2)


def device_of(pos, core):
    return (pos[Z] * 8 + pos[X] * 2 + core, pos[Y])


def moved(pos, axis, step):
    out = list(pos)
    out[axis] = lax.rem(pos[axis] + step, 4)
    return out


def enter(pos, core):
    barrier = pltpu.get_barrier_semaphore()
    other = 1 - core
    peers = [device_of(pos, other)]
    for axis in (Z, X, Y):
        for step in (1, 2, 3):
            for c in (core, other):
                peers.append(device_of(moved(pos, axis, step), c))
    for peer in peers:
        pl.semaphore_signal(barrier, inc=1, device_id=peer, device_id_type=MESH)
    pl.semaphore_wait(barrier, len(peers))


def remote(src, dst, send_sem, recv_sem, device):
    return pltpu.make_async_remote_copy(
        src_ref=src,
        dst_ref=dst,
        send_sem=send_sem,
        recv_sem=recv_sem,
        device_id=device,
        device_id_type=MESH,
    )


def drain(ref, sem):
    pltpu.make_async_copy(ref, ref, sem).wait()


def part_of(pos, i):
    return lax.rem(pos[Y] + 1 + i, 4)


def start_one(t, pos, core, src, dst, sems, i):
    axis = ORDERS[t][0]
    mine = pos[axis]
    yy = part_of(pos, i)
    send, recv = sems[0].at[0], sems[1].at[t]
    for step in (1, 3, 2, 0):
        for flip in (0, 1):
            c = core if flip == 0 else 1 - core
            to = moved(pos, axis, step)
            if t == 0:
                a, b = src.at[to[axis], c, :, yy], dst.at[mine, core, :, yy]
            else:
                a, b = src.at[to[axis], c, yy], dst.at[mine, core, yy]
            if step == 0 and flip == 0:
                local = pltpu.make_async_copy(a, b, recv)
            else:
                remote(a, b, send, recv, device_of(to, c)).start()
    local.start()


def start_one_y(pos, core, src, dst, sems, step, flips=(0, 1)):
    mine = pos[Y]
    to = moved(pos, Y, step)
    for flip in flips:
        c = core if flip == 0 else 1 - core
        remote(src.at[to[Y], c], dst.at[mine, core], sems[0].at[0], sems[1].at[2], device_of(to, c)).start()


def start_part(pos, core, src, dst, sems, i):
    for t in (0, 1):
        start_one(t, pos, core, src[t], dst[t], sems, i)

    @pl.when(i < 3)
    def _():
        start_one_y(pos, core, src[2], dst[2], sems, i + 1)

    @pl.when(i == 3)
    def _():
        start_one_y(pos, core, src[2], dst[2], sems, 0, (1,))
        pltpu.make_async_copy(
            src[2].at[pos[Y], core], dst[2].at[pos[Y], core], sems[1].at[2]
        ).start()


def start_two(t, pos, core, src, dst, sems):
    axis = ORDERS[t][1]
    mine = pos[axis]
    send, recv = sems[0].at[1], sems[1].at[3 + t]
    for step in (1, 3, 2):
        to = moved(pos, axis, step)
        remote(src.at[:, :, to[axis]], dst.at[mine], send, recv, device_of(to, core)).start()
    pltpu.make_async_copy(src.at[:, :, mine], dst.at[mine], recv).start()


def start_three(t, pos, core, src, dst, sems, recvs):
    axis = ORDERS[t][2]
    mine = pos[axis]
    for step in (1, 3, 2):
        to = moved(pos, axis, step)
        remote(src.at[:, :, :, to[axis]], dst.at[mine], sems[0].at[2], recvs[step], device_of(to, core)).start()
    pltpu.make_async_copy(src.at[:, :, :, mine], dst.at[mine], recvs[0]).start()


def wait_all(copies):
    for copy in copies:
        copy.wait()


def place(order, z, x, y):
    pos = (z, x, y)
    return pos[order[0]], pos[order[1]], pos[order[2]]


def build_matrices(taps_ref, line_ref, plane_ref):
    distance = (
        lax.broadcasted_iota(jnp.int32, (SIDE, SIDE), 0)
        - lax.broadcasted_iota(jnp.int32, (SIDE, SIDE), 1)
        + TAPS // 2
    )
    taps = taps_ref[...].astype(F32)
    table = jnp.zeros((SIDE, SIDE), F32)
    for t in range(TAPS):
        table = jnp.where(distance == t, jnp.broadcast_to(taps[:, t : t + 1], (SIDE, SIDE)), table)
    table = table.astype(BF16)

    def chosen(index):
        lanes = lax.broadcasted_iota(jnp.int32, (256, SIDE), 1)
        return jnp.where(index == lanes, 1.0, 0.0).astype(BF16)

    def spread(a, b):
        first = jnp.dot(a, table, preferred_element_type=F32).astype(BF16)
        return lax.dot_general(first, b, (((1,), (1,)), ((), ())), preferred_element_type=F32)

    place_of = lax.broadcasted_iota(jnp.int32, (256, SIDE), 0)
    rows = lax.broadcasted_iota(jnp.int32, (256, 256), 0)
    cols = lax.broadcasted_iota(jnp.int32, (256, 256), 1)
    table_in = [chosen((place_of >> 4) + 16 * b) for b in range(2)]
    same = (rows & 15) == (cols & 15)
    for b_out in range(2):
        first = lax.dot_general(
            table_in[b_out], table, (((1,), (1,)), ((), ())), preferred_element_type=F32
        ).astype(BF16)
        for b_in in range(2):
            value = lax.dot_general(
                first, table_in[b_in], (((1,), (1,)), ((), ())), preferred_element_type=F32
            )
            line_ref[b_out * 256 : b_out * 256 + 256, b_in * 256 : b_in * 256 + 256] = jnp.where(
                same, value, 0.0
            ).astype(BF16)
    same = (rows & 31) == (cols & 31)
    centre = chosen((place_of >> 5) + 8)
    for shift in (-1, 0, 1):
        value = jnp.where(same, spread(chosen((place_of >> 5) + 8 + 8 * shift), centre), 0.0)
        if shift == 0:
            inner = spread(chosen(place_of & 31), chosen(place_of & 31))
            value = value + jnp.where((rows >> 5) == (cols >> 5), inner, 0.0)
        value = value.astype(BF16)
        nothing = jnp.zeros_like(value)
        for c in range(4):
            inside = 0 <= c + shift < 4
            plane_ref[c, (shift + 1) * 256 : (shift + 2) * 256, :] = value if inside else nothing


def refine_half(fh, cc, refs):
    fn_ref, params_ref, pot_ref, line_ref, plane_ref, acc_ref, r_ref, send = refs
    c0 = pl.multiple_of(cc * 256, 256)
    cm = pl.multiple_of(jnp.maximum(cc - 1, 0) * 256, 256)
    cp = pl.multiple_of(jnp.minimum(cc + 1, 3) * 256, 256)

    def stacked(f0, offset):
        return jnp.concatenate(
            [fn_ref[f0 : f0 + 16, pl.ds(pl.multiple_of(x * 1024 + offset, 256), 256)] for x in range(SIDE)],
            axis=0,
        )

    for fl in range(2):
        f0 = fh * 32 + fl * 16
        own = stacked(f0, c0)
        acc = jnp.dot(line_ref[...], own, preferred_element_type=F32)
        acc += jnp.dot(stacked(f0, cm), plane_ref[cc, 0:256, :], preferred_element_type=F32)
        acc += jnp.dot(own, plane_ref[cc, 256:512, :], preferred_element_type=F32)
        acc += jnp.dot(stacked(f0, cp), plane_ref[cc, 512:768, :], preferred_element_type=F32)
        acc_ref[fl] = acc

    lane_block = lax.broadcasted_iota(jnp.int32, (16, 256), 1) >> 6
    column = []
    for fl in range(2):
        f0 = fh * 32 + fl * 16
        energy = jnp.broadcast_to(params_ref[f0 : f0 + 16, 0:1], (16, 256))
        first = jnp.broadcast_to(params_ref[f0 : f0 + 16, 1:2], (16, 256)).astype(jnp.int32)
        last = jnp.broadcast_to(params_ref[f0 : f0 + 16, 2:3], (16, 256)).astype(jnp.int32)
        first = first - lane_block
        last = last - lane_block
        column.append((energy, 0.3 / (1.0 - energy), first, last))

    def refined(x, fl):
        f0 = fh * 32 + fl * 16
        energy, step, first, last = column[fl]
        at = pl.ds(pl.multiple_of(x * 1024 + c0, 256), 256)
        value = fn_ref[f0 : f0 + 16, at].astype(F32)
        kinetic = acc_ref[fl, pl.ds(x * 16, 16), :]
        row = x * 8 + cc * 2
        potential = jnp.concatenate([pot_ref[pl.ds(row, 1), :], pot_ref[pl.ds(row + 1, 1), :]], axis=1)
        gradient = kinetic + (potential - energy) * value
        value = value - step * gradient
        block = x * 16 + cc * 4
        inside = (first <= block) & (last > block)
        value = jnp.where(inside, value, 0.0)
        r_ref[f0 : f0 + 16, at] = value.astype(BF16)
        return value

    low = lax.broadcasted_iota(jnp.int32, (16, 128), 1) < 64
    for xs in range(16):
        z, x = xs // 4, xs % 4
        for fl in range(2):
            value = refined(xs + 8, fl).astype(BF16)
            for h in range(2):
                a1, a2, a3 = place(ORDERS[fh], z, x, cc)
                send[fh][a1, h, a2, a3, fl * 16 : fl * 16 + 16, :] = value[:, h * 128 : h * 128 + 128]
    for xd in range(8):
        folded = [refined(xd, fl) + refined(xd + 24, fl) for fl in range(2)]
        for h in range(2):
            z, x = xd // 2, (xd % 2) * 2 + h
            a, b = (part[:, h * 128 : h * 128 + 128] for part in folded)
            a1, a2, a3 = place(ORDERS[2], z, x, cc)
            first = jnp.where(low, a, pltpu.roll(b, 64, 1))
            second = jnp.where(low, pltpu.roll(a, 64, 1), b)
            send[2][a1, 0, a2, a3, fh * 16 : fh * 16 + 16, :] = first.astype(BF16)
            send[2][a1, 1, a2, a3, fh * 16 : fh * 16 + 16, :] = second.astype(BF16)


def unpack_halves(piece):
    low = lax.broadcasted_iota(jnp.int32, (16, 128), 1) < 64
    parts = []
    for fh in range(2):
        p = piece[fh * 16 : fh * 16 + 16].astype(F32)
        q = pltpu.roll(p, 64, 1)
        parts.append(jnp.where(low, p, q))
        parts.append(jnp.where(low, q, p))
    return jnp.concatenate(parts, axis=0)


def split(g):
    return g >> 5, (g >> 3) & 3, (g >> 2) & 1, g & 3


def orthonormalize(
    partners_ref, fn_hbm, taps_ref, energy_ref, start_ref, length_ref, pot_ref,
    f0_hbm, f1_hbm, f2_hbm, r_hbm, own_ref,
    fn_ref, line_ref, plane_ref, acc_ref, r_ref, square_ref, params_ref, first_ref,
    e0, e1, e2, a0, a1, a2, b0, b1, b2, g0, g1, g2, st_a, st_b, st_c,
    after_ref, u_ref,
    q0, q1, q2, p0, p1, p2, m0, m1, m2, t0, t1, t2, n0, n1, n2, v0, v1, v2,
    k0, k1, k2, l0, l1, l2, c0, c1, c2,
    s0, s1, s2, h0, h1, h2, i0, i1, i2,
    load_sem, store_sem, in_send, in_recv, st_send, st_recv, r_send, r_recv, g_send, g_recv, x_send, x_recv,
    o_send, o_recv,
):
    pos, core = position()
    load = pltpu.make_async_copy(fn_hbm, fn_ref, load_sem)
    load.start()
    enter(pos, core)

    first_ref[...] = jnp.zeros((1, 128), F32)
    first_ref[0:1, 0:GROUP] = start_ref[...].astype(F32)
    starts = []
    for step in range(4):
        for flip in range(2):
            c = core if flip == 0 else 1 - core
            index = step * 2 + flip
            dst = st_a.at[pos[Z], core]
            if index == 0:
                starts.append(pltpu.make_async_copy(first_ref, dst, st_recv.at[0]))
            else:
                starts.append(
                    remote(first_ref, dst, st_send.at[index], st_recv.at[0], device_of(moved(pos, Z, step), c))
                )

    square_ref[...] = jnp.zeros((128, 128), F32)
    square_ref[0:1, 0:GROUP] = energy_ref[...]
    square_ref[1:2, 0:GROUP] = start_ref[...].astype(F32)
    square_ref[2:3, 0:GROUP] = (start_ref[...] + length_ref[...]).astype(F32)
    params_ref[...] = jnp.transpose(square_ref[...])[0:GROUP]
    build_matrices(taps_ref, line_ref, plane_ref)
    for copy in starts:
        copy.start()
    load.wait()
    send, one, two, got = (e0, e1, e2), (a0, a1, a2), (b0, b1, b2), (g0, g1, g2)
    sems = (in_send, in_recv)
    refs = (fn_ref, params_ref, pot_ref, line_ref, plane_ref, acc_ref, r_ref, send)

    def refine(i, carry):
        for fh in range(2):
            refine_half(fh, part_of(pos, i), refs)
        start_part(pos, core, send, one, sems, i)
        return carry

    lax.fori_loop(0, 4, refine, 0)
    store = pltpu.make_async_copy(r_ref, r_hbm, store_sem)
    store.start()

    sent = starts[1:]
    drain(st_a, st_recv.at[0])
    starts = []
    for step in range(4):
        dst = st_b.at[pos[X]]
        if step == 0:
            starts.append(pltpu.make_async_copy(st_a, dst, st_recv.at[1]))
        else:
            starts.append(remote(st_a, dst, st_send.at[8 + step], st_recv.at[1], device_of(moved(pos, X, step), core)))
    for copy in starts:
        copy.start()

    for t in range(3):
        drain(one[t], in_recv.at[t])
        start_two(t, pos, core, one[t], two[t], sems)
    sent += starts[1:]
    drain(st_b, st_recv.at[1])
    starts = []
    for step in range(4):
        dst = st_c.at[pos[Y]]
        if step == 0:
            starts.append(pltpu.make_async_copy(st_b, dst, st_recv.at[2]))
        else:
            starts.append(remote(st_b, dst, st_send.at[12 + step], st_recv.at[2], device_of(moved(pos, Y, step), core)))
    for copy in starts:
        copy.start()

    def own_part(i, total):
        rows = r_ref[:, pl.ds(pl.multiple_of(i * 1024, 1024), 1024)]
        return total + lax.dot_general(
            rows, rows, (((1,), (1,)), ((), ())), preferred_element_type=F32
        )

    total = lax.fori_loop(0, NC // 1024, own_part, jnp.zeros((GROUP, GROUP), F32))
    unit = lax.broadcasted_iota(jnp.int32, (GROUP, GROUP), 0) == lax.broadcasted_iota(
        jnp.int32, (GROUP, GROUP), 1
    )
    own = 0.5 * (total * (1.0 / (BLOCK * LMAX)) - jnp.where(unit, 1.0, 0.0))
    own_ref[...] = own.astype(BF16)

    for t in (2, 0, 1):
        drain(two[t], in_recv.at[3 + t])
        recvs = [in_recv.at[8 + step] if t == 2 else in_recv.at[6 + t] for step in range(4)]
        start_three(t, pos, core, two[t], got[t], sems, recvs)

    sent += starts[1:]
    drain(st_c, st_recv.at[2])
    for i in range(128):
        y, x, z, c = i >> 5, (i >> 3) & 3, (i >> 1) & 3, i & 1
        square_ref[z * 32 + x * 8 + c * 4 + y : z * 32 + x * 8 + c * 4 + y + 1, :] = st_c[y, x, z, c]
    block = (pos[Z] * 2 + lax.div(pos[X], 2)) * 16 + pos[Y] * 4 + lax.rem(pos[X], 2) * 2 + core
    above = jnp.where(square_ref[...] > block.astype(F32), 1.0, 0.0)
    after_ref[...] = jnp.transpose(above)[0:GROUP]

    lower = lax.broadcasted_iota(jnp.int32, (GROUP, 128), 1) < 64

    for step in (0, 1, 3, 2):
        x = lax.rem(pos[X] + 4 - step, 4)
        drain(g2.at[x], in_recv.at[8 + step])

        def unfold(j, carry, x=x):
            z, y, c = j >> 3, (j >> 1) & 3, j & 1
            g = z * 32 + x * 8 + c * 4 + y
            folded = unpack_halves(g2[x, z, y, c])
            turned = pltpu.roll(after_ref[...], lax.rem(128 - g, 128), 1)
            upper = jnp.broadcast_to(turned[:, 0:1], (GROUP, 128)) > 0.5
            keep = jnp.logical_xor(upper, lower)
            u_ref[g] = jnp.where(keep, folded, 0.0).astype(BF16)
            return carry

        lax.fori_loop(0, 32, unfold, 0, unroll=4)
    drain(g0, in_recv.at[6])
    drain(g1, in_recv.at[7])

    def columns(g):
        z, x, c, y = split(g)
        return jnp.concatenate(
            [jnp.concatenate([g0[y, x, z, c], g1[z, y, x, c]], axis=0), u_ref[g]], axis=1
        )

    def partners(g):
        return jnp.concatenate([columns(partners_ref[k, g]) for k in range(3)], axis=0)

    half_low = lax.broadcasted_iota(jnp.int32, (32, 128), 1) < 64
    q, p, m = (q0, q1, q2), (p0, p1, p2), (m0, m1, m2)
    t, n, v = (t0, t1, t2), (n0, n1, n2), (v0, v1, v2)
    sums = (r_send, r_recv)

    def intersect_part(i, carry):
        y = part_of(pos, i)

        def intersect(j, inner):
            z, x, c = j >> 3, (j >> 1) & 3, j & 1
            g = z * 32 + x * 8 + c * 4 + y
            part = lax.dot_general(
                columns(g), partners(g), (((1,), (1,)), ((), ())), preferred_element_type=F32
            )
            q0[z, c, x, y] = part[0:32, 0:128].astype(BF16)
            q1[x, c, y, z] = part[32:64, 0:128].astype(BF16)
            last = jnp.concatenate([part[:, 128:192], part[:, 128:192]], axis=1)
            q2[y, c, z, x] = jnp.where(half_low, last[0:32], last[32:64]).astype(BF16)
            return inner

        lax.fori_loop(0, 32, intersect, 0, unroll=4)
        start_part(pos, core, q, p, sums, i)
        return carry

    lax.fori_loop(0, 4, intersect_part, 0)

    orders = ORDERS
    for i in range(3):
        drain(p[i], r_recv.at[i])
        for j in range(4):
            total = p[i][0, 0, j].astype(F32)
            for k in range(1, 8):
                total += p[i][k >> 1, k & 1, j].astype(F32)
            m[i][j] = total.astype(BF16)
        axis = orders[i][1]
        for step in range(1, 4):
            to = moved(pos, axis, step)
            remote(m[i].at[to[axis]], t[i].at[step - 1], r_send.at[1], r_recv.at[3 + i], device_of(to, core)).start()
    for i in range(3):
        drain(t[i], r_recv.at[3 + i])
        total = m[i][pos[orders[i][1]]].astype(F32)
        for k in range(3):
            total += t[i][k].astype(F32)
        n[i][...] = total.astype(BF16)
        axis = orders[i][2]
        for step in range(1, 4):
            to = moved(pos, axis, step)
            remote(n[i].at[to[axis]], v[i].at[step - 1], r_send.at[2], r_recv.at[6 + i], device_of(to, core)).start()

    kk, ll, cp = (k0, k1, k2), (l0, l1, l2), (c0, c1, c2)
    for i in range(3):
        drain(v[i], r_recv.at[6 + i])
        axis = orders[i][2]
        mine = pos[axis]
        total = n[i][mine].astype(F32)
        for k in range(3):
            total += v[i][k].astype(F32)
        kk[i][mine] = (0.5 * (total * (1.0 / (BLOCK * LMAX)))).astype(BF16)
        for step in range(1, 4):
            to = device_of(moved(pos, axis, step), core)
            remote(kk[i].at[mine], kk[i].at[mine], g_send.at[0], g_recv.at[i], to).start()
    for i in range(3):
        drain(v[i], g_recv.at[i])
        axis = orders[i][1]
        mine = pos[axis]
        pltpu.make_async_copy(kk[i], ll[i].at[mine], g_recv.at[3 + i]).start()
        for step in range(1, 4):
            to = device_of(moved(pos, axis, step), core)
            remote(kk[i], ll[i].at[mine], g_send.at[1], g_recv.at[3 + i], to).start()
    for i in range(3):
        drain(ll[i], g_recv.at[3 + i])
        axis = orders[i][0]
        mine = pos[axis]
        pltpu.make_async_copy(ll[i], cp[i].at[mine, core], g_recv.at[6 + i * 4]).start()
        for step in range(1, 4):
            to = device_of(moved(pos, axis, step), core)
            remote(ll[i], cp[i].at[mine, core], g_send.at[2], g_recv.at[6 + i * 4 + step], to).start()
    for step in (0, 1, 3, 2):
        for i in range(3):
            at = lax.rem(pos[orders[i][0]] + 4 - step, 4)
            here = cp[i].at[at, core]
            drain(here, g_recv.at[6 + i * 4 + step])
            remote(here, here, x_send, x_recv.at[i], device_of(pos, 1 - core)).start()
    for i in range(3):
        drain(cp[i].at[:, 1 - core], x_recv.at[i])

    s, back, turn, out = (s0, s1, s2), (h0, h1, h2), (i0, i1, i2), (f0_hbm, f1_hbm, f2_hbm)
    sems = (o_send, o_recv)

    def shift_part(i, carry):
        y = part_of(pos, i)

        def shift(j, inner):
            z, x, c = j >> 3, (j >> 1) & 3, j & 1
            g = z * 32 + x * 8 + c * 4 + y
            third = c2[y, c, z, x]
            third = jnp.concatenate([third[:, 0:64], third[:, 64:128]], axis=0)
            pair = jnp.concatenate([c0[z, c, x, y], c1[x, c, y, z]], axis=0)
            weights = jnp.concatenate([pair, third], axis=1)
            moved_by = jnp.dot(weights, partners(g), preferred_element_type=F32).astype(BF16)
            s0[z, c, x, y] = moved_by[0:48, 0:128]
            s1[x, c, y, z] = moved_by[0:48, 128:256]
            s2[y, c, z, x, 0:16] = moved_by[48:64, 0:128]
            s2[y, c, z, x, 16:32] = moved_by[48:64, 128:256]
            return inner

        lax.fori_loop(0, 32, shift, 0, unroll=4)
        start_part(pos, core, s, back, sems, i)
        return carry

    lax.fori_loop(0, 4, shift_part, 0)
    for i in range(3):
        drain(back[i], o_recv.at[i])
        start_two(i, pos, core, back[i], turn[i], sems)
    for i in range(3):
        drain(turn[i], o_recv.at[3 + i])
        start_three(i, pos, core, turn[i], out[i], sems, [o_recv.at[6 + i]] * 4)

    def sent_all(sem, pieces):
        drain(fn_ref.at[:, 0 : pieces * 64], sem)

    store.wait()
    for copy in sent:
        copy.wait_send()
    for sem_set in (in_send, r_send):
        sent_all(sem_set.at[0], 3 * 7 * 16)
    for stage in (1, 2):
        sent_all(in_send.at[stage], 3 * 3 * 32)
    few = e0.at[0:3, 0, 0:3]
    one_each = e0.at[0:3, 0, 0:3, 0]
    drain(few, r_send.at[1])
    drain(one_each, r_send.at[2])
    drain(one_each, g_send.at[0])
    drain(few, g_send.at[1])
    sent_all(g_send.at[2], 3 * 3 * 16)
    sent_all(x_send, 3 * 4 * 16)
    sent_all(o_send.at[0], 4 * 7 * 16)
    sent_all(o_send.at[1], 4 * 3 * 32)
    sent_all(o_send.at[2], 4 * 3 * 32)
    for i in range(3):
        drain(out[i], o_recv.at[6 + i])


ROWS = (48, 48, 32)


def run_orthonormalize(
    functions, filter_taps, potential, energies, region_start, region_length, partner_groups
):
    anywhere = pl.BlockSpec(memory_space=pltpu.HBM)
    whole = pl.BlockSpec(memory_space=pltpu.VMEM)
    dma = pltpu.SemaphoreType.DMA

    def vmem(*shape, kind=BF16):
        return pltpu.VMEM(shape, kind)

    return pl.pallas_call(
        orthonormalize,
        out_shape=tuple(jax.ShapeDtypeStruct((4, 4, 4, 2, r, 128), BF16) for r in ROWS)
        + (jax.ShapeDtypeStruct((GROUP, NC), BF16), jax.ShapeDtypeStruct((GROUP, GROUP), BF16)),
        in_specs=[pl.BlockSpec(memory_space=pltpu.SMEM), anywhere] + [whole] * 5,
        out_specs=(anywhere,) * 4 + (whole,),
        scratch_shapes=[
            vmem(GROUP, NC),
            vmem(512, 512),
            vmem(4, 768, 256),
            vmem(2, 512, 256, kind=F32),
            vmem(GROUP, NC),
            vmem(128, 128, kind=F32),
            vmem(GROUP, 128, kind=F32),
            vmem(1, 128, kind=F32),
        ]
        + [vmem(4, 2, 4, 4, 32, 128)] * 6
        + [vmem(4, 4, 2, 4, 32, 128)] * 3
        + [vmem(4, 4, 4, 2, 32, 128)] * 3
        + [vmem(4, 2, 1, 128, kind=F32), vmem(4, 4, 2, 1, 128, kind=F32), vmem(4, 4, 4, 2, 1, 128, kind=F32)]
        + [vmem(GROUP, 128, kind=F32), vmem(128, GROUP, 128)]
        + [vmem(4, 2, 4, 4, 32, 128)] * 6
        + [vmem(4, 4, 32, 128)] * 3
        + [vmem(3, 4, 32, 128)] * 3
        + [vmem(4, 32, 128)] * 3
        + [vmem(3, 32, 128)] * 3
        + [vmem(4, 32, 128)] * 3
        + [vmem(4, 4, 32, 128)] * 3
        + [vmem(4, 2, 4, 4, 32, 128)] * 3
        + [vmem(4, 2, 4, 4, r, 128) for r in ROWS]
        + [vmem(4, 2, 4, 4, r, 128) for r in ROWS]
        + [vmem(4, 4, 2, 4, r, 128) for r in ROWS]
        + [dma, dma, dma((3,)), dma((12,)), dma((16,)), dma((3,)), dma((3,)), dma((9,))]
        + [dma((3,)), dma((18,)), dma, dma((3,)), dma((3,)), dma((9,))],
        compiler_params=pltpu.CompilerParams(
            collective_id=0, has_side_effects=True, vmem_limit_bytes=63 * 1024 * 1024
        ),
    )(
        partner_groups.T,
        functions,
        filter_taps.reshape(1, TAPS),
        energies.reshape(1, GROUP),
        region_start.reshape(1, GROUP),
        region_length.reshape(1, GROUP),
        potential.reshape(256, 128),
    )


def finish(own_ref, r_hbm, f0_hbm, f1_hbm, f2_hbm, o_hbm, r_ref, f0_ref, f1_ref, f2_ref, o_ref, in_sem, out_sem):
    weights = own_ref[...]
    low = lax.broadcasted_iota(jnp.int32, (GROUP, 128), 1) < 64

    def loads(i):
        z, x = lax.div(i, 2), lax.rem(i, 2) * 2
        pairs = []
        for k, (slab, count) in enumerate(((i, 1), (i + 24, 1), (8 + 2 * i, 2))):
            cut = pl.ds(pl.multiple_of(slab * 1024, 1024), count * 1024)
            pairs.append((r_hbm.at[:, cut], r_ref.at[:, cut]))
        cut = pl.ds(x, 2)
        pairs.append((f0_hbm.at[:, cut, z], f0_ref.at[:, cut, z]))
        pairs.append((f1_hbm.at[z, :, cut], f1_ref.at[z, :, cut]))
        pairs.append((f2_hbm.at[cut, z], f2_ref.at[cut, z]))
        return [pltpu.make_async_copy(a, b, in_sem.at[i]) for a, b in pairs]

    def stores(i):
        out = []
        for k, (slab, count) in enumerate(((i, 1), (i + 24, 1), (8 + 2 * i, 2))):
            cut = pl.ds(pl.multiple_of(slab * 1024, 1024), count * 1024)
            out.append(pltpu.make_async_copy(o_ref.at[:, cut], o_hbm.at[:, cut], out_sem))
        return out

    def each(make):
        def body(i, carry):
            for copy in make(i):
                copy.start()
            return carry

        return body

    lax.fori_loop(0, 8, each(loads), 0)

    def slab_part(slab, y, moved_by):
        at = pl.ds(pl.multiple_of(slab * 1024 + y * 256, 256), 256)
        rows = r_ref[:, at]
        shifted = jnp.dot(weights, rows, preferred_element_type=F32)
        moved_by = jnp.concatenate(moved_by, axis=1)
        o_ref[:, at] = (rows.astype(F32) - shifted - moved_by).astype(BF16)

    def step(i, carry):
        drain(r_ref.at[:, 0:8192], in_sem.at[i])
        z, x0 = lax.div(i, 2), lax.rem(i, 2) * 2
        for y in range(4):
            lows, highs = [], []
            for dx in range(2):
                x = x0 + dx
                ones, twos = [], []
                for c in range(2):
                    tail = f2_ref[x, z, y, c].astype(F32)
                    ones.append(jnp.concatenate([f0_ref[y, x, z, c].astype(F32), tail[0:16]], axis=0))
                    twos.append(jnp.concatenate([f1_ref[z, y, x, c].astype(F32), tail[16:32]], axis=0))
                slab_part(8 + 2 * i + dx, y, ones)
                turned = [pltpu.roll(two, 64, 1) for two in twos]
                lows.append(jnp.where(low, twos[0], turned[1]))
                highs.append(jnp.where(low, turned[0], twos[1]))
            slab_part(i, y, lows)
            slab_part(i + 24, y, highs)
        for copy in stores(i):
            copy.start()
        return carry

    lax.fori_loop(0, 8, step, 0)

    drain(o_ref, out_sem)


def run_finish(own, refined, f0, f1, f2):
    anywhere = pl.BlockSpec(memory_space=pltpu.HBM)
    return pl.pallas_call(
        finish,
        out_shape=jax.ShapeDtypeStruct((GROUP, NC), BF16),
        in_specs=[pl.BlockSpec(memory_space=pltpu.VMEM)] + [anywhere] * 4,
        out_specs=anywhere,
        scratch_shapes=[pltpu.VMEM((GROUP, NC), BF16)]
        + [pltpu.VMEM((4, 4, 4, 2, r, 128), BF16) for r in ROWS]
        + [pltpu.VMEM((GROUP, NC), BF16), pltpu.SemaphoreType.DMA((8,)), pltpu.SemaphoreType.DMA],
        compiler_params=pltpu.CompilerParams(vmem_limit_bytes=63 * 1024 * 1024),
    )(own, refined, f0, f1, f2)


def on_device(functions, filter_taps, potential, energies, region_start, region_length, partner_groups):
    f0, f1, f2, refined, own = run_orthonormalize(
        functions, filter_taps, potential, energies, region_start, region_length, partner_groups
    )
    return run_finish(own, refined, f0, f1, f2)


def solution(mesh):
    return jax.shard_map(
        on_device,
        mesh=mesh,
        in_specs=(
            P(("grid", "rep"), None),
            P(),
            P(),
            P(("grid", "rep")),
            P(("grid", "rep")),
            P(("grid", "rep")),
            P(),
        ),
        out_specs=P(("grid", "rep"), None),
        check_vma=False,
    )
```
